256 devices in a mesh: head: 16 (over z_hi, y, core), tail: 16 (over z_lo, x).
Axes of the slice: x: 4, y: 4, z: 8 (z_hi: 2, z_lo: 4; z = z_hi * 4 + z_lo), core: 2. Of those that a mesh axis runs over, the one named last changes fastest.
Arguments:
- head_table: float32 [131072, 512], P(('head', 'tail')), may hold values from -2.5 to 2.5
- head_state: float32 [131072], P(('head', 'tail')), may hold values from 0.01 to 0.1
- tail_table: float32 [131072, 512], P(('head', 'tail')), may hold values from -2.5 to 2.5
- tail_state: float32 [131072], P(('head', 'tail')), may hold values from 0.01 to 0.1
- relations: float32 [1024, 512], P(('head', 'tail')), may hold values from -0.25 to 0.25
- relation_state: float32 [1024, 512], P(('head', 'tail')), may hold values from 10 to 100
- head_rows: int32 [2, 131072], P(None, ('head', 'tail')), may hold values from 0 to 511
- tail_rows: int32 [2, 131072], P(None, ('head', 'tail')), may hold values from 0 to 511
- negatives: int32 [2, 1024, 128], P(None, ('head', 'tail')), may hold values from 0 to 511
- relation_ids: int32 [2, 1024], P(None, ('head', 'tail')), may hold values from 0 to 1
- block_counts: int32 [2, 256], P(None, ('head', 'tail')), may hold values from 1 to 4, 512 in all within a row
Outputs:
- heads_out: float32 [131072, 512], P(('head', 'tail'))
- tails_out: float32 [131072, 512], P(('head', 'tail'))
- relations_out: float32 [1024, 512], P(('head', 'tail'))
The draws below stay inside these ranges and needn't reach their ends.
Inputs may be any that keep to these rules, and one draw needn't show every extreme that they name: `block_counts`: in each bucket the counts over all devices sum to 4 // 2 times the number of devices, and some device has 4.
All inputs are finite; a program needn't handle non-finite values.
Results may differ from the reference program's by a relative error of at most 0.01.
Values may be sent and summed in bfloat16 or wider, within the bound.
A program may use at most 64 MiB of HBM per device.

```python
import math
import jax
import jax.numpy as jnp
import numpy as np
from jax import lax

D = 512
NREL = 2
BLOCK = 128
NNEG = 128
EB = 4
HROWS = 512
TROWS = 512
HEAD_ENTITIES = 131072
TAIL_ENTITIES = 131072
EDGE_SLOTS = 131072
EDGE_BLOCKS = 1024
N_HEAD = 16
N_TAIL = 16
DEVICES = 256


def plant(result, key, low, high):
    spot = [jax.random.randint(jax.random.fold_in(key, axis), (), 0, length) for axis, length in enumerate(result.shape)]
    longest = result.shape.index(max(result.shape))
    neighbour = spot[:longest] + [(spot[longest] + 1) % result.shape[longest]] + spot[longest + 1:]
    return result.at[tuple(spot)].set(low).at[tuple(neighbour)].set(high)


def block_levels(stream_key, extent, cuts, low, largest):
    def one(axis_at, shards_of):
        heights = jax.random.uniform(jax.random.fold_in(jax.random.fold_in(stream_key, 6), axis_at), (shards_of,), jnp.float32, low / len(cuts), largest / len(cuts))
        return jnp.repeat(jnp.exp(heights), extent[axis_at] // shards_of).reshape((-1,) + (1,) * (len(extent) - axis_at - 1))

    factor_of = one(*cuts[0])
    for cut in cuts[1:]:
        factor_of = factor_of * one(*cut)
    return factor_of


def length_profile(count, total, reach, lean):
    loads = [(1 << 20) // math.isqrt(rank ** lean) + 1 for rank in range(2, count + 1)]
    surplus, given = total - reach - (count - 1), [1] * (count - 1)
    while surplus > 0:
        free = [i for i in range(count - 1) if given[i] < reach]
        mass, remaining = sum([loads[i] for i in free]), surplus
        for i in free:
            extra = min(reach - given[i], max(1, remaining * loads[i] // mass), surplus)
            given[i] = given[i] + extra
            surplus = surplus - extra
    return np.array([reach] + given)


def ragged_sizes(rng, amount, total, bound, slope):
    if amount == 2:
        one = jax.random.randint(rng, (), max(1, total - bound), min(bound, total - 1) + 1)
        return jnp.stack([one, total - one])
    lengths = jnp.asarray(length_profile(amount, total, bound, slope), jnp.int32)
    pairs = (amount - 1) // 2
    donor, taker = lengths[1:1 + 2 * pairs:2], lengths[2:2 + 2 * pairs:2]
    margin = jnp.minimum(donor - 1, bound - taker)
    passed = jax.random.randint(jax.random.fold_in(rng, 1), (pairs,), 0, 1 << 20) % (margin + 1)
    lengths = lengths.at[1:1 + 2 * pairs:2].set(donor - passed).at[2:2 + 2 * pairs:2].set(taker + passed)
    return lengths[jax.random.permutation(jax.random.fold_in(rng, 2), amount)]


def noise(rng, extent, width, limit, cuts=(), kind=jnp.bfloat16):
    drawn = jax.random.normal(rng, extent, jnp.float32) * width
    if len(cuts) > 0:
        drawn = block_levels(rng, extent, cuts, -0.22, 0.18) * drawn
    return jnp.clip(drawn, min=-limit, max=limit).astype(kind)


def setup_inputs(seed: int = 0) -> dict:
    key_list = jax.random.split(jax.random.key(seed), 12)
    return {
        "head_table": noise(key_list[0], (HEAD_ENTITIES, D), 0.3, 2.5, ((0, 256),), jnp.float32),
        "head_state": jnp.clip(jnp.exp(math.log(0.1) - 2.3025851 * jax.random.uniform(key_list[1], (HEAD_ENTITIES,), jnp.float32) ** block_levels(key_list[1], (HEAD_ENTITIES,), ((0, 256),), -0.2, 0.2)), 0.01, 0.1),
        "tail_table": noise(key_list[2], (TAIL_ENTITIES, D), 0.3, 2.5, ((0, 256),), jnp.float32),
        "tail_state": jnp.clip(jnp.exp(math.log(0.1) - 2.3025851 * jax.random.uniform(key_list[3], (TAIL_ENTITIES,), jnp.float32) ** block_levels(key_list[3], (TAIL_ENTITIES,), ((0, 256),), -0.2, 0.2)), 0.01, 0.1),
        "relations": noise(key_list[4], (NREL * D, D), D ** -0.5, 0.25, ((0, 256),), jnp.float32),
        "relation_state": jnp.clip(jnp.exp(math.log(100.0) - 2.3025851 * jax.random.uniform(key_list[5], (NREL * D, D), jnp.float32) ** block_levels(key_list[5], (NREL * D, D), ((0, 256),), -0.2, 0.2)), 10.0, 100.0),
        "head_rows": plant(jax.random.randint(key_list[6], (2, EDGE_SLOTS), 0, HROWS), jax.random.fold_in(key_list[6], 1), 0, HROWS - 1).astype(jnp.int32),
        "tail_rows": plant(jax.random.randint(key_list[7], (2, EDGE_SLOTS), 0, TROWS), jax.random.fold_in(key_list[7], 1), 0, TROWS - 1).astype(jnp.int32),
        "negatives": plant(jax.random.randint(key_list[8], (2, EDGE_BLOCKS, NNEG), 0, TROWS), jax.random.fold_in(key_list[8], 1), 0, TROWS - 1).astype(jnp.int32),
        "relation_ids": plant(jax.random.randint(key_list[9], (2, EDGE_BLOCKS), 0, NREL), jax.random.fold_in(key_list[9], 1), 0, NREL - 1).astype(jnp.int32),
        "block_counts": jax.vmap(lambda own: ragged_sizes(own, DEVICES, (EB // 2) * DEVICES, EB, 2))(jax.random.split(key_list[10], 2)).reshape((2, DEVICES)).astype(jnp.int32),
    }


RATE_ROWS = 0.2
RATE_RELATIONS = 0.05
EPSILON = 1e-06

def row_adagrad(emb_table, row_state, gradient):
    state_new = row_state + lax.optimization_barrier(jnp.mean(gradient * gradient, axis=1))
    table_new = emb_table - RATE_ROWS * gradient / (jnp.sqrt(state_new) + EPSILON)[:, None]
    return (table_new, state_new)

def relation_adagrad(rel_table, rel_state, gradient):
    state_new = rel_state + gradient * gradient
    return (rel_table - RATE_RELATIONS * gradient / (jnp.sqrt(state_new) + EPSILON), state_new)

def score_bucket(head_table, head_state, tail_table, tail_state, rel_bf, head_index, tail_index, neg_index, rel_index, live_blocks):
    model_width = head_table.shape[1]
    block_total = rel_index.shape[0]
    per_block = head_index.shape[0] // block_total
    neg_total = neg_index.shape[1]
    rel_total = rel_bf.shape[0] // model_width
    head_vecs = head_table[head_index].astype(jnp.bfloat16).reshape(block_total, per_block, model_width)
    tail_vecs = tail_table[tail_index].astype(jnp.bfloat16).reshape(block_total, per_block, model_width)
    neg_vecs = tail_table[neg_index].astype(jnp.bfloat16)
    chosen = rel_bf.reshape(rel_total, model_width, model_width)[rel_index]
    live_mask = (jnp.arange(block_total, dtype=jnp.int32) < live_blocks).astype(jnp.float32)
    chosen_wide = chosen.astype(jnp.float32)
    projected = jnp.einsum('bed,bdk->bek', head_vecs.astype(jnp.float32), chosen_wide).astype(jnp.bfloat16)
    proj_wide = projected.astype(jnp.float32)
    tail_wide = tail_vecs.astype(jnp.float32)
    neg_wide = neg_vecs.astype(jnp.float32)
    pos_score = jnp.einsum('bek,bek->be', proj_wide, tail_wide)
    neg_score = jnp.einsum('bek,bnk->ben', proj_wide, neg_wide)
    pos_weight = -jax.nn.sigmoid(-pos_score) * live_mask[:, None]
    neg_weight = (jax.nn.sigmoid(neg_score) * live_mask[:, None, None] / neg_total).astype(jnp.bfloat16)
    neg_weight_wide = neg_weight.astype(jnp.float32)
    edge_grad = (pos_weight[:, :, None] * tail_wide + jnp.einsum('ben,bnk->bek', neg_weight_wide, neg_wide)).astype(jnp.bfloat16)
    head_terms = jnp.einsum('bek,bdk->bed', edge_grad.astype(jnp.float32), chosen_wide).reshape(-1, model_width)
    head_grad = jnp.zeros(head_table.shape, jnp.float32).at[head_index].add(head_terms)
    pos_terms = (pos_weight[:, :, None] * proj_wide).reshape(-1, model_width)
    neg_terms = jnp.einsum('ben,bek->bnk', neg_weight_wide, proj_wide).reshape(-1, model_width)
    tail_grad = jnp.zeros(tail_table.shape, jnp.float32).at[tail_index].add(pos_terms)
    tail_grad = tail_grad.at[neg_index.reshape(-1)].add(neg_terms)
    head_new, head_state_new = row_adagrad(head_table, head_state, head_grad)
    tail_new, tail_state_new = row_adagrad(tail_table, tail_state, tail_grad)
    onehot = (rel_index[:, None] == jnp.arange(rel_total, dtype=jnp.int32)[None, :]).astype(jnp.bfloat16)
    spread = (head_vecs[:, :, None, :] * onehot[:, None, :, None]).reshape(-1, rel_total * model_width)
    grad_term = jnp.dot(spread.T, edge_grad.reshape(-1, model_width), preferred_element_type=jnp.float32)
    return (head_new, head_state_new, tail_new, tail_state_new, grad_term)

def run_bucket(rel_bf, head_table, head_state, tail_table, tail_state, head_index, tail_index, neg_index, rel_index, live_blocks):

    def per_device(grad_sum, pieces):
        results = score_bucket(pieces[0], pieces[1], pieces[2], pieces[3], rel_bf, pieces[4], pieces[5], pieces[6], pieces[7], pieces[8])
        return (grad_sum + results[4], (results[0], results[1], results[2], results[3]))
    zero_sum = jnp.zeros((rel_bf.shape[0], rel_bf.shape[1]), jnp.float32)
    grad_sum, blocks = lax.scan(per_device, zero_sum, (head_table, head_state, tail_table, tail_state, head_index, tail_index, neg_index, rel_index, live_blocks))
    return (grad_sum, blocks)

def reference(head_table, head_state, tail_table, tail_state, relations, relation_state, head_rows, tail_rows, negatives, relation_ids, block_counts):
    devices_all = N_HEAD * N_TAIL
    slots = EB * BLOCK
    head_blocks = head_table.reshape(devices_all, HROWS, D)
    head_states = head_state.reshape(devices_all, HROWS)
    tail_blocks = tail_table.reshape(devices_all, TROWS, D)
    tail_states = tail_state.reshape(devices_all, TROWS)
    rel_table = relations
    rel_state = relation_state
    for bucket in range(2):
        if bucket == 1:
            tail_blocks = jnp.roll(tail_blocks.reshape(N_HEAD, N_TAIL, TROWS, D), 1, axis=1).reshape(devices_all, TROWS, D)
            tail_states = jnp.roll(tail_states.reshape(N_HEAD, N_TAIL, TROWS), 1, axis=1).reshape(devices_all, TROWS)
        rel_bf = rel_table.astype(jnp.bfloat16)
        grad_sum, blocks = run_bucket(rel_bf, head_blocks, head_states, tail_blocks, tail_states, head_rows[bucket].reshape(devices_all, slots), tail_rows[bucket].reshape(devices_all, slots), negatives[bucket].reshape(devices_all, EB, NNEG), relation_ids[bucket].reshape(devices_all, EB), block_counts[bucket])
        head_blocks, head_states, tail_blocks, tail_states = blocks
        rel_table, rel_state = relation_adagrad(rel_table, rel_state, grad_sum)
    return (head_blocks.reshape(-1, D), tail_blocks.reshape(-1, D), rel_table)
```

```python
import functools

import jax
import jax.numpy as jnp
from jax import lax
from jax.experimental import pallas as pl
from jax.experimental.pallas import tpu as pltpu
from jax.sharding import PartitionSpec as P

MESH = pl.DeviceIdType.MESH
RATE_ROWS = 0.2
RATE_RELATIONS = 0.05
EPSILON = 1e-06
D = 512
EB = 4
BLOCK = 128
F32 = jnp.float32
BF16 = jnp.bfloat16
VMEM = pl.BlockSpec(memory_space=pltpu.VMEM)
SMEM = pl.BlockSpec(memory_space=pltpu.SMEM)


def place():
    hd, tl = lax.axis_index("head"), lax.axis_index("tail")
    return dict(
        core=hd % 2, y=(hd // 2) % 4, z=(hd // 8) * 4 + tl // 4, x=tl % 4
    )


def device(core, y, z, x):
    return ((z // 4) * 8 + y * 2 + core, (z % 4) * 4 + x)


def peers_of(w):
    out = [dict(w, core=1 - w["core"])]
    out += [dict(w, x=(w["x"] + d) % 4) for d in range(1, 4)]
    out += [dict(w, y=(w["y"] + d) % 4) for d in range(1, 4)]
    out += [dict(w, z=(w["z"] + d) % 8) for d in range(1, 8)]
    return [device(**o) for o in out]


def greet(w, extra=()):
    barrier = pltpu.get_barrier_semaphore()
    everyone = peers_of(w) + list(extra)
    for peer in everyone:
        pl.semaphore_signal(barrier, inc=1, device_id=peer, device_id_type=MESH)
    pl.semaphore_wait(barrier, len(everyone))


def send(src, dst, ssem, rsem, to):
    copy = pltpu.make_async_remote_copy(
        src_ref=src, dst_ref=dst, send_sem=ssem, recv_sem=rsem, device_id=to, device_id_type=MESH
    )
    copy.start()
    return copy


def finish(copies):
    for copy in copies:
        copy.wait()


def mine(w, shape):
    row = lax.broadcasted_iota(jnp.int32, shape, 0)
    return row // 4 == w["x"] % 2


def gather_relations(w, tile8, xsrc, xbuf, rel, ssem, rsem):
    x, y, z, core = w["x"], w["y"], w["z"], w["core"]
    xsrc[...] = tile8
    copies = []
    for d in range(1, 4):
        copies.append(
            send(xsrc, xbuf.at[x], ssem.at[d], rsem.at[d], device(**dict(w, x=(x + d) % 4)))
        )
    xbuf[x] = tile8
    finish(copies)
    low = (xbuf[0] + xbuf[1]).astype(BF16)
    high = (xbuf[2] + xbuf[3]).astype(BF16)
    rel[z // 4, y, core, z % 4] = jnp.concatenate([low, high], axis=0)
    here = rel.at[z // 4, y, core, z % 4]
    copies = []
    for d in range(1, 8):
        copies.append(
            send(here, here, ssem.at[3 + d], rsem.at[3 + d], device(**dict(w, z=(z + d) % 8)))
        )
    finish(copies)
    here = rel.at[:, y, core]
    copies = []
    for d in range(1, 4):
        copies.append(
            send(here, here, ssem.at[10 + d], rsem.at[10 + d], device(**dict(w, y=(y + d) % 4)))
        )
    finish(copies)
    here = rel.at[:, :, core]
    finish([send(here, here, ssem.at[14], rsem.at[14], device(**dict(w, core=1 - core)))])


AG_SCRATCH = [
    pltpu.VMEM((8, D), F32),
    pltpu.VMEM((4, 8, D), F32),
    pltpu.SemaphoreType.DMA((15,)),
    pltpu.SemaphoreType.DMA((15,)),
]


def scatter_gradient(w, g, cbuf, psrc, ybuf, zsrc, zbuf, xs, xr, ssem, rsem):
    x, y, z, core = w["x"], w["y"], w["z"], w["core"]
    finish(
        [send(g.at[:, :, 1 - core], cbuf, ssem.at[14], rsem.at[14], device(**dict(w, core=1 - core)))]
    )
    copies = []
    for d in range(1, 4):
        to = (y + d) % 4
        psrc[d - 1] = (g[:, to, core].astype(F32) + cbuf[:, to].astype(F32)).astype(BF16)
        copies.append(
            send(psrc.at[d - 1], ybuf.at[d - 1], ssem.at[d], rsem.at[d], device(**dict(w, y=to)))
        )
    own = g[:, y, core].astype(F32) + cbuf[:, y].astype(F32)
    finish(copies)
    own = own + ybuf[0].astype(F32) + ybuf[1].astype(F32) + ybuf[2].astype(F32)
    zsrc[...] = own.reshape(8, 16, D)
    copies = []
    for d in range(1, 8):
        to = (z + d) % 8
        zb = zsrc[to].astype(BF16)
        zbuf[6 + d] = zb
        copies.append(
            send(zbuf.at[6 + d], zbuf.at[d - 1], ssem.at[3 + d], rsem.at[3 + d], device(**dict(w, z=to)))
        )
    own = zsrc[z]
    finish(copies)
    for d in range(7):
        own = own + zbuf[d].astype(F32)
    xs[...] = own.reshape(2, 8, D)
    copies = []
    for d in range(1, 4):
        to = (x + d) % 4
        copies.append(
            send(xs.at[to // 2], xr.at[d - 1], ssem.at[10 + d], rsem.at[10 + d], device(**dict(w, x=to)))
        )
    own = xs[x // 2]
    finish(copies)
    return own + xr[0] + xr[1] + xr[2]


RS_SCRATCH = [
    pltpu.VMEM((2, 4, 4, 16, D), BF16),
    pltpu.VMEM((3, 2, 4, 16, D), BF16),
    pltpu.VMEM((3, 2, 4, 16, D), BF16),
    pltpu.VMEM((8, 16, D), F32),
    pltpu.VMEM((14, 16, D), BF16),
    pltpu.VMEM((2, 8, D), F32),
    pltpu.VMEM((3, 8, D), F32),
    pltpu.SemaphoreType.DMA((15,)),
    pltpu.SemaphoreType.DMA((15,)),
]


def relation_step(rel, state, grad):
    state = state + grad * grad
    return rel - RATE_RELATIONS * grad / (jnp.sqrt(state) + EPSILON), state


def twice(ref4, ref8):
    ref8[0:4, :] = ref4[...]
    ref8[4:8, :] = ref4[...]


def first_kernel(rel4, rel, rel8, xsrc, xbuf, ssem, rsem):
    w = place()
    twice(rel4, rel8)
    greet(w)
    tile8 = jnp.where(mine(w, (8, D)), rel8[...], 0.0)
    gather_relations(w, tile8, xsrc, xbuf, rel, ssem, rsem)


def middle_kernel(
    g, rel4, st4, tail, tstate, rel, rel8, st8, tail_out, tstate_out, *scratch
):
    rs, ag, (shift_s, shift_r) = scratch[:9], scratch[9:13], scratch[13:]
    w = place()
    hd, tl = lax.axis_index("head"), lax.axis_index("tail")
    right, left = (hd, (tl + 1) % 16), (hd, (tl + 15) % 16)
    twice(rel4, rel8)
    twice(st4, st8)
    greet(w, (right, left))
    moved = [
        send(tail, tail_out, shift_s.at[0], shift_r.at[0], right),
        send(tstate, tstate_out, shift_s.at[1], shift_r.at[1], right),
    ]
    grad = scatter_gradient(w, g, *rs)
    new, state = relation_step(rel8[...], st8[...], grad)
    keep = mine(w, (8, D))
    new = jnp.where(keep, new, 0.0)
    rel8[...] = new
    st8[...] = jnp.where(keep, state, 1.0)
    gather_relations(w, new, ag[0], ag[1], rel, ag[2], ag[3])
    finish(moved)


def last_kernel(g, rel8, st8, out4, *scratch):
    w = place()
    greet(w)
    grad = scatter_gradient(w, g, *scratch)
    new, _ = relation_step(rel8[...], st8[...], grad)
    out4[...] = jnp.where(w["x"] % 2 == 0, new[0:4], new[4:8])


def selectors(idx_row):
    wide = jnp.broadcast_to(idx_row, (BLOCK, BLOCK))
    col = wide.T
    lane = lax.broadcasted_iota(jnp.int32, (BLOCK, BLOCK), 1)
    picks = [jnp.where(col == lane + BLOCK * j, 1.0, 0.0) for j in range(4)]
    pick = jnp.concatenate(picks, axis=1).astype(BF16)
    row = lax.broadcasted_iota(jnp.int32, (D, BLOCK), 0)
    put = jnp.where(row == jnp.broadcast_to(idx_row, (D, BLOCK)), 1.0, 0.0).astype(BF16)
    return pick, put


def dot(a, b):
    return jnp.dot(a, b, preferred_element_type=F32)


def dot_nt(a, b):
    return lax.dot_general(a, b, (((1,), (1,)), ((), ())), preferred_element_type=F32)


def dot_tn(a, b):
    return lax.dot_general(a, b, (((0,), (0,)), ((), ())), preferred_element_type=F32)


def as_column(row):
    return jnp.broadcast_to(row, (BLOCK, D)).T


def as_row(col):
    return jnp.broadcast_to(col, (D, BLOCK)).T[0:1, :]


def row_update(table, state_row, grad, out, state_out):
    state = as_column(state_row)[:, 0:1] + jnp.mean(grad * grad, axis=1, keepdims=True)
    out[...] = (table - grad * (RATE_ROWS / (jnp.sqrt(state) + EPSILON))).astype(out.dtype)
    if state_out is not None:
        state_out[...] = as_row(state)


def bucket_kernel(
    k, head, hstate, tail, tstate, rel, hrows, trows, negs, rids, counts, *rest
):
    last = k == 1
    if last:
        head_out, tail_out, g = rest[:3]
        hstate_out = tstate_out = None
        rest = rest[3:]
    else:
        head_out, hstate_out, tail_out, tstate_out, g = rest[:5]
        rest = rest[5:]
    hb, tb, h, t, n, u, gu, hput, tput, terms = rest
    hb[...] = head[...].astype(BF16)
    tb[...] = tail[...].astype(BF16)
    for b in range(EB):
        rows = pl.ds(b * BLOCK, BLOCK)
        pick, put = selectors(hrows[k : k + 1, b * BLOCK : (b + 1) * BLOCK])
        h[rows, :] = dot(pick, hb[...]).astype(BF16)
        hput[:, b * BLOCK : (b + 1) * BLOCK] = put
        pick, put = selectors(trows[k : k + 1, b * BLOCK : (b + 1) * BLOCK])
        t[rows, :] = dot(pick, tb[...]).astype(BF16)
        tput[:, b * BLOCK : (b + 1) * BLOCK] = put
        pick, put = selectors(negs[k, b : b + 1, :])
        n[rows, :] = dot(pick, tb[...]).astype(BF16)
        tput[:, D + b * BLOCK : D + (b + 1) * BLOCK] = put
    for b in range(EB):
        rows = pl.ds(b * BLOCK, BLOCK)
        live = (b < counts[k, 0]).astype(F32)
        one = (rids[k, b] == 1).astype(F32)
        chosen = jnp.where(rids[k, b] == 1, rel[D:, :], rel[:D, :])
        ub = dot(h[rows, :], chosen).astype(BF16)
        u[rows, :] = ub
        tf = t[rows, :].astype(F32)
        uf = ub.astype(F32)
        pos = jnp.sum(uf * tf, axis=1, keepdims=True)
        gp = -live * jax.nn.sigmoid(-pos)
        neg = dot_nt(ub, n[rows, :])
        gn = (live * jax.nn.sigmoid(neg) / BLOCK).astype(BF16)
        gub = (gp * tf + dot(gn, n[rows, :])).astype(BF16)
        gu[rows, 0:D] = (gub.astype(F32) * (1.0 - one)).astype(BF16)
        gu[rows, D:] = (gub.astype(F32) * one).astype(BF16)
        terms[rows, :] = (gp * uf).astype(BF16)
        terms[D + b * BLOCK : D + (b + 1) * BLOCK, :] = dot_tn(gn, ub).astype(BF16)
    g[0:D, :] = dot_tn(h[...], gu[:, 0:D]).astype(BF16)
    g[D:, :] = dot_tn(h[...], gu[:, D:]).astype(BF16)
    tgrad = dot(tput[...], terms[...])
    row_update(tail[...].astype(F32), tstate[...], tgrad, tail_out, tstate_out)
    hterms = dot_nt(gu[:, 0:D], rel[:D, :]) + dot_nt(gu[:, D:], rel[D:, :])
    hgrad = dot(hput[...], hterms.astype(BF16))
    row_update(head[...], hstate[...], hgrad, head_out, hstate_out)


def bucket(k, *args):
    table = jax.ShapeDtypeStruct((D, D), F32)
    state = jax.ShapeDtypeStruct((1, D), F32)
    grad = jax.ShapeDtypeStruct((2 * D, D), BF16)
    tail = jax.ShapeDtypeStruct((D, D), BF16)
    outs = (table, table, grad) if k == 1 else (table, state, tail, state, grad)
    return pl.pallas_call(
        functools.partial(bucket_kernel, k),
        name=f"bucket{k}",
        out_shape=outs,
        in_specs=[VMEM] * 8 + [SMEM] * 2,
        out_specs=[VMEM] * len(outs),
        scratch_shapes=[
            pltpu.VMEM((D, D), BF16),
            pltpu.VMEM((D, D), BF16),
            pltpu.VMEM((D, D), BF16),
            pltpu.VMEM((D, D), BF16),
            pltpu.VMEM((D, D), BF16),
            pltpu.VMEM((D, D), BF16),
            pltpu.VMEM((D, 2 * D), BF16),
            pltpu.VMEM((D, D), BF16),
            pltpu.VMEM((D, 2 * D), BF16),
            pltpu.VMEM((2 * D, D), BF16),
        ],
        compiler_params=pltpu.CompilerParams(vmem_limit_bytes=48 << 20),
    )(*args)


def comm(body, name, number, outs, n_in, scratch):
    return pl.pallas_call(
        body,
        name=name,
        out_shape=outs,
        in_specs=[VMEM] * n_in,
        out_specs=[VMEM] * len(outs),
        scratch_shapes=scratch,
        compiler_params=pltpu.CompilerParams(
            collective_id=number, has_side_effects=True, vmem_limit_bytes=32 << 20
        ),
    )


def shards(
    head_table,
    head_state,
    tail_table,
    tail_state,
    relations,
    relation_state,
    head_rows,
    tail_rows,
    negatives,
    relation_ids,
    block_counts,
):
    full = jax.ShapeDtypeStruct((2, 4, 2, 4, 16, D), BF16)
    tile = jax.ShapeDtypeStruct((8, D), F32)
    hstate, tstate = head_state.reshape(1, D), tail_state.reshape(1, D)
    index = (head_rows, tail_rows, negatives, relation_ids, block_counts)
    (rel,) = comm(
        first_kernel, "first", 1, (full,), 1, [pltpu.VMEM((8, D), F32)] + AG_SCRATCH
    )(relations)
    head, hstate, tail, tstate, grad = bucket(
        0, head_table, hstate, tail_table, tstate, rel.reshape(2 * D, D), *index
    )
    rel, rel8, st8, tail, tstate = comm(
        middle_kernel,
        "middle",
        2,
        (
            full,
            tile,
            tile,
            jax.ShapeDtypeStruct((D, D), BF16),
            jax.ShapeDtypeStruct((1, D), F32),
        ),
        5,
        RS_SCRATCH + AG_SCRATCH + [pltpu.SemaphoreType.DMA((2,)), pltpu.SemaphoreType.DMA((2,))],
    )(grad.reshape(full.shape), relations, relation_state, tail, tstate)
    heads_out, tails_out, grad = bucket(
        1, head, hstate, tail, tstate, rel.reshape(2 * D, D), *index
    )
    (relations_out,) = comm(
        last_kernel, "last", 3, (jax.ShapeDtypeStruct((4, D), F32),), 3, RS_SCRATCH
    )(grad.reshape(full.shape), rel8, st8)
    return heads_out, tails_out, relations_out


def solution(mesh):
    both = ("head", "tail")
    in_specs = (
        P(both, None),
        P(both),
        P(both, None),
        P(both),
        P(both, None),
        P(both, None),
        P(None, both),
        P(None, both),
        P(None, both, None),
        P(None, both),
        P(None, both),
    )
    out_specs = (P(both, None), P(both, None), P(both, None))
    return jax.shard_map(shards, mesh=mesh, in_specs=in_specs, out_specs=out_specs, check_vma=False)
```

```python
import jax
import jax.numpy as jnp
from jax import lax
from jax.experimental import pallas as pl
from jax.experimental.pallas import tpu as pltpu
from jax.sharding import PartitionSpec as P

MESH = pl.DeviceIdType.MESH
RATE_ROWS = 0.2
RATE_RELATIONS = 0.05
EPSILON = 1e-06
D = 512
EB = 4
BLOCK = 128
F32 = jnp.float32
BF16 = jnp.bfloat16
I32 = jnp.int32
VMEM = pl.BlockSpec(memory_space=pltpu.VMEM)
ANY = pl.BlockSpec(memory_space=pl.ANY)


class Place:
    def __init__(self):
        hd, tl = lax.axis_index("head"), lax.axis_index("tail")
        self.core, self.y, self.x = hd % 2, (hd // 2) % 4, tl % 4
        self.z = (hd // 8) * 4 + tl // 4
        self.right, self.left = (hd, (tl + 1) % 16), (hd, (tl + 15) % 16)

    def at(self, core=None, y=None, z=None, x=None):
        core = self.core if core is None else core
        y = self.y if y is None else y
        z = self.z if z is None else z
        x = self.x if x is None else x
        return ((z // 4) * 8 + y * 2 + core, (z % 4) * 4 + x)

    def partner(self):
        return self.at(core=1 - self.core)

    def xd(self, d):
        return (self.x + d) % 4

    def yd(self, d):
        return (self.y + d) % 4

    def zd(self, d):
        return (self.z + d) % 8


def signal_peers(w):
    barrier = pltpu.get_barrier_semaphore()
    peers = [w.partner(), w.right, w.left]
    peers += [w.at(x=w.xd(d)) for d in range(1, 4)]
    peers += [w.at(y=w.yd(d)) for d in range(1, 4)]
    peers += [w.at(z=w.zd(d)) for d in range(1, 8)]
    for peer in peers:
        pl.semaphore_signal(barrier, inc=1, device_id=peer, device_id_type=MESH)
    return barrier, len(peers)


def remote(src, dst, ssem, rsem, to):
    return pltpu.make_async_remote_copy(
        src_ref=src, dst_ref=dst, send_sem=ssem, recv_sem=rsem, device_id=to, device_id_type=MESH
    )


def send(src, dst, ssem, rsem, to):
    copy = remote(src, dst, ssem, rsem, to)
    copy.start()
    return copy


NEAR = (1, 7, 2, 6, 3, 5, 4)
FAR = (4, 3, 5, 2, 6, 1, 7)


def gather_tiles(w, rel, sems, segments):
    zs, zr, ys, yr, cs, cr = sems
    late = []

    def tile(z, y, core):
        return rel.at[z // 4, y, core, z % 4]

    def to_core(t):
        send(t, t, cs.at[0], cr.at[0], w.partner())

    def spread(d):
        t = tile(w.zd(8 - d), w.y, w.core)
        for e in (2, 1, 3):
            late.append(send(t, t, ys.at[e - 1, d], yr.at[e - 1, d], w.at(y=w.yd(e))))
        to_core(t)

    def arrive_z(d):
        t = tile(w.zd(8 - d), w.y, w.core)
        remote(t, t, zs.at[d - 1], zr.at[d - 1], w.partner()).wait_recv()
        spread(d)

    def arrive_y(d):
        for e in (1, 3, 2):
            t = tile(w.zd(8 - d), w.yd(4 - e), w.core)
            remote(t, t, ys.at[e - 1, d], yr.at[e - 1, d], w.partner()).wait_recv()
            to_core(t)

    own = tile(w.z, w.y, w.core)
    for d in FAR:
        late.append(send(own, own, zs.at[d - 1], zr.at[d - 1], w.at(z=w.zd(d))))
    spread(0)
    segments[0]()
    for d in (1, 7, 2, 6):
        arrive_z(d)
    arrive_y(0)
    arrive_z(3)
    arrive_z(5)
    arrive_z(4)
    segments[1]()
    for d in NEAR:
        arrive_y(d)
    other = rel.at[:, :, 1 - w.core]
    half = rel.at[:, :, w.core]
    remote(other, other, cs.at[0], cr.at[0], w.partner()).wait_recv()
    remote(half, half, cs.at[0], cr.at[0], w.partner()).wait_send()
    for copy in late:
        copy.wait_send()


AG_SEMS = [(7,), (7,), (3, 8), (3, 8), (1,), (1,)]


def reduce_tiles(w, g, bufs, sems, segments):
    cbuf, psrc, ybuf, acc, zsrc, zbuf, xt = bufs
    cs, cr, ys, yr, zs, zr, xs, xr = sems
    late = []
    order = FAR + (0,)
    for d in order:
        z = w.zd(d)
        late.append(
            send(g.at[z // 4, :, 1 - w.core, z % 4], cbuf.at[d], cs.at[d], cr.at[d], w.partner())
        )
    for d in order:
        z = w.zd(d)
        remote(cbuf.at[d], cbuf.at[d], cs.at[d], cr.at[d], w.partner()).wait_recv()
        for e in (2, 1, 3):
            y = w.yd(e)
            both = g[z // 4, y, w.core, z % 4].astype(F32) + cbuf[d, y].astype(F32)
            psrc[e - 1, d] = both.astype(BF16)
            late.append(
                send(psrc.at[e - 1, d], ybuf.at[e - 1, d], ys.at[e - 1, d], yr.at[e - 1, d], w.at(y=y))
            )
        acc[d] = g[z // 4, w.y, w.core, z % 4].astype(F32) + cbuf[d, w.y].astype(F32)
    segments[0]()
    total = None
    for d in order:
        total = acc[d]
        for e in (1, 3, 2):
            remote(
                ybuf.at[e - 1, d], ybuf.at[e - 1, d], ys.at[e - 1, d], yr.at[e - 1, d], w.partner()
            ).wait_recv()
            total = total + ybuf[e - 1, d].astype(F32)
        if d > 0:
            zsrc[d - 1] = total.astype(BF16)
            late.append(
                send(zsrc.at[d - 1], zbuf.at[d - 1], zs.at[d - 1], zr.at[d - 1], w.at(z=w.zd(d)))
            )
    acc[0] = total
    segments[1]()
    total = acc[0]
    for d in NEAR:
        remote(
            zbuf.at[d - 1], zbuf.at[d - 1], zs.at[d - 1], zr.at[d - 1], w.partner()
        ).wait_recv()
        total = total + zbuf[d - 1].astype(F32)
    xt[w.x] = total.astype(BF16)
    for e in (2, 1, 3):
        late.append(
            send(xt.at[w.x], xt.at[w.x], xs.at[e - 1], xr.at[e - 1], w.at(x=w.xd(e)))
        )
    segments[2]()
    for e in (1, 3, 2):
        t = xt.at[w.xd(4 - e)]
        remote(t, t, xs.at[e - 1], xr.at[e - 1], w.partner()).wait_recv()
    total = xt[0].astype(F32) + xt[1].astype(F32) + xt[2].astype(F32) + xt[3].astype(F32)
    return total, late


RS_SEMS = [(8,), (8,), (3, 8), (3, 8), (7,), (7,), (3,), (3,)]
RS_BUFS = [
    pltpu.VMEM((8, 4, 16, D), BF16),
    pltpu.VMEM((3, 8, 16, D), BF16),
    pltpu.VMEM((3, 8, 16, D), BF16),
    pltpu.VMEM((8, 16, D), F32),
    pltpu.VMEM((7, 16, D), BF16),
    pltpu.VMEM((7, 16, D), BF16),
    pltpu.VMEM((4, 16, D), BF16),
]


def dot(a, b):
    return jnp.dot(a, b, preferred_element_type=F32)


def dot_nt(a, b):
    return lax.dot_general(a, b, (((1,), (1,)), ((), ())), preferred_element_type=F32)


def dot_tn(a, b):
    return lax.dot_general(a, b, (((0,), (0,)), ((), ())), preferred_element_type=F32)


def selectors(idx_row):
    wide = jnp.broadcast_to(idx_row, (BLOCK, BLOCK))
    col = wide.T
    lane = lax.broadcasted_iota(I32, (BLOCK, BLOCK), 1)
    picks = [jnp.where(col == lane + BLOCK * j, 1.0, 0.0) for j in range(4)]
    pick = jnp.concatenate(picks, axis=1).astype(BF16)
    row = lax.broadcasted_iota(I32, (D, BLOCK), 0)
    put = jnp.where(row == jnp.broadcast_to(idx_row, (D, BLOCK)), 1.0, 0.0).astype(BF16)
    return pick, put


def block(b):
    return slice(b * BLOCK, (b + 1) * BLOCK)


def pick_rows(index_of, table, out, put, base):
    for b in range(EB):
        pick, place = selectors(index_of(b))
        out[block(b), :] = dot(pick, table[...]).astype(BF16)
        put[:, base + b * BLOCK : base + (b + 1) * BLOCK] = place


def as_column(row):
    return jnp.broadcast_to(row, (BLOCK, D)).T


def as_row(col):
    return jnp.broadcast_to(col, (D, BLOCK)).T[0:1, :]


def row_update(table, state_row, grad):
    state = as_column(state_row)[:, 0:1] + jnp.mean(grad * grad, axis=1, keepdims=True)
    return table - grad * (RATE_ROWS / (jnp.sqrt(state) + EPSILON)), state


def relation_step(rel, state, grad):
    state = state + grad * grad
    return rel - RATE_RELATIONS * grad / (jnp.sqrt(state) + EPSILON), state


def kernel(
    rel4_in, st4_in, head_in, hstate_in, tail_in, tstate_in,
    hrows_in, trows_in, negs_in, rids_in, counts_in,
    head_out, tail_out, rel_out,
    rel4, st4, head, hstate, tail, tstate, hrows, trows, negs, rids, counts,
    rel8, st8, xsrc, xbuf, rel16, st16, rel_a, rel_b, g_a, g_b,
    hb, tb, h, t, n, u, gu, gn, hput, tput, terms, tnew, tmoved, tsnew, tsmoved,
    load, xsem_s, xsem_r, msem_s, msem_r, *more,
):
    rs_bufs = [more[0:7], more[7:14]]
    more = more[14:]
    ag_sems = [more[0:6], more[6:12]]
    rs_sems = [more[12:20], more[20:28]]
    w = Place()
    barrier, peers = signal_peers(w)
    ins = (rel4_in, st4_in, hrows_in, head_in, rids_in, counts_in, tail_in, trows_in, negs_in,
           hstate_in, tstate_in)
    outs = (rel4, st4, hrows, head, rids, counts, tail, trows, negs, hstate, tstate)
    loads = []
    for i, (a, b) in enumerate(zip(ins, outs)):
        copy = pltpu.make_async_copy(a, b, load.at[i])
        copy.start()
        loads.append(copy)

    def loaded(*which):
        for i in which:
            loads[i].wait()

    def pick_head(k):
        hb[...] = head[...].astype(BF16)
        pick_rows(lambda b: hrows[k : k + 1, block(b)], hb, h, hput, 0)

    def pick_tail(k):
        pick_rows(lambda b: trows[k : k + 1, block(b)], tb, t, tput, 0)

    def pick_negs(k):
        pick_rows(lambda b: negs[k, b : b + 1, :], tb, n, tput, D)

    def score(k, rel, g):
        r0, r1 = rel[0].reshape(D, D), rel[1].reshape(D, D)
        for b in range(EB):
            rows = block(b)
            live = (b < counts[k]).astype(F32)
            one = (rids[k, b] == 1).astype(F32)
            ub = dot(h[rows, :], jnp.where(rids[k, b] == 1, r1, r0)).astype(BF16)
            u[rows, :] = ub
            tf = t[rows, :].astype(F32)
            uf = ub.astype(F32)
            gp = -live * jax.nn.sigmoid(-jnp.sum(uf * tf, axis=1, keepdims=True))
            gnb = (live * jax.nn.sigmoid(dot_nt(ub, n[rows, :])) / BLOCK).astype(BF16)
            gn[rows, :] = gnb
            gub = (gp * tf + dot(gnb, n[rows, :])).astype(BF16).astype(F32)
            gu[rows, 0:D] = (gub * (1.0 - one)).astype(BF16)
            gu[rows, D:] = (gub * one).astype(BF16)
            terms[rows, :] = (gp * uf).astype(BF16)
        g[0] = dot_tn(h[...], gu[:, 0:D]).astype(BF16).reshape(4, 2, 4, 16, D)
        g[1] = dot_tn(h[...], gu[:, D:]).astype(BF16).reshape(4, 2, 4, 16, D)

    def tail_grad():
        for b in range(EB):
            rows = block(b)
            terms[D + b * BLOCK : D + (b + 1) * BLOCK, :] = dot_tn(gn[rows, :], u[rows, :]).astype(BF16)
        return dot(tput[...], terms[...])

    def head_grad(rel):
        r0, r1 = rel[0].reshape(D, D), rel[1].reshape(D, D)
        hterms = dot_nt(gu[:, 0:D], r0) + dot_nt(gu[:, D:], r1)
        return dot(hput[...], hterms.astype(BF16))

    nothing = lambda: None

    loaded(0, 1, 2, 3)
    rel8[0:4, :] = rel4[...]
    rel8[4:8, :] = rel4[...]
    st8[0:4, :] = st4[...]
    st8[4:8, :] = st4[...]
    mine = lax.broadcasted_iota(I32, (8, D), 0) // 4 == w.x % 2
    xsrc[0] = jnp.where(mine, rel8[...], 0.0)
    xsrc[1] = jnp.where(mine, st8[...], 0.0)
    pick_head(0)
    pl.semaphore_wait(barrier, peers)
    xsends = []
    for part in range(2):
        for e in (2, 1, 3):
            xsends.append(
                send(
                    xsrc.at[part], xbuf.at[part, w.x],
                    xsem_s.at[part, e - 1], xsem_r.at[part, e - 1], w.at(x=w.xd(e)),
                )
            )
        xbuf[part, w.x] = xsrc[part]
    loaded(6, 7)
    tb[...] = tail[...].astype(BF16)
    pick_tail(0)

    def merge(part, out):
        for e in (1, 3, 2):
            to = xbuf.at[part, w.xd(4 - e)]
            remote(
                to, to, xsem_s.at[part, e - 1], xsem_r.at[part, e - 1], w.partner()
            ).wait_recv()
        out[0:8, :] = xbuf[part, 0] + xbuf[part, 1]
        out[8:16, :] = xbuf[part, 2] + xbuf[part, 3]

    merge(0, rel16)
    rel_a[w.z // 4, w.y, w.core, w.z % 4] = rel16[...].astype(BF16)

    def negs_first():
        loaded(8)
        pick_negs(0)

    gather_tiles(w, rel_a, ag_sems[0], (negs_first, nothing))
    loaded(4, 5, 9, 10)

    score(0, rel_a, g_a)
    moved = []

    def tail_step():
        new, state = row_update(tail[...], tstate[...], tail_grad())
        tnew[...] = new.astype(BF16)
        tsnew[...] = as_row(state)
        moved.append(send(tnew, tmoved, msem_s.at[0], msem_r.at[0], w.right))
        moved.append(send(tsnew, tsmoved, msem_s.at[1], msem_r.at[1], w.right))

    def head_step():
        new, state = row_update(head[...], hstate[...], head_grad(rel_a))
        head[...] = new
        hstate[...] = as_row(state)

    grad, late = reduce_tiles(
        w, g_a, rs_bufs[0], rs_sems[0], (tail_step, head_step, lambda: pick_head(1))
    )
    merge(1, st16)
    new, state = relation_step(rel16[...], st16[...], grad)
    rel16[...] = new
    st16[...] = state
    rel_b[w.z // 4, w.y, w.core, w.z % 4] = new.astype(BF16)

    def tail_arrives():
        for copy in moved:
            copy.wait()
        pick_rows(lambda b: trows[1:2, block(b)], tmoved, t, tput, 0)

    gather_tiles(
        w, rel_b, ag_sems[1],
        (tail_arrives, lambda: pick_rows(lambda b: negs[1, b : b + 1, :], tmoved, n, tput, D)),
    )

    score(1, rel_b, g_b)

    def tail_last():
        new, _ = row_update(tmoved[...].astype(F32), tsmoved[...], tail_grad())
        tail_out[...] = new

    def head_last():
        new, _ = row_update(head[...], hstate[...], head_grad(rel_b))
        head_out[...] = new

    grad, later = reduce_tiles(
        w, g_b, rs_bufs[1], rs_sems[1], (tail_last, head_last, nothing)
    )
    new, _ = relation_step(rel16[...], st16[...], grad)
    out = new[0:4]
    for i in range(1, 4):
        out = jnp.where(w.x == i, new[4 * i : 4 * i + 4], out)
    rel_out[...] = out
    for copy in xsends + late + later:
        copy.wait_send()


def dma(shape):
    return pltpu.SemaphoreType.DMA(shape)


def shards(
    head_table,
    head_state,
    tail_table,
    tail_state,
    relations,
    relation_state,
    head_rows,
    tail_rows,
    negatives,
    relation_ids,
    block_counts,
):
    table = jax.ShapeDtypeStruct((D, D), F32)
    args = (
        relations, relation_state, head_table, head_state.reshape(1, D), tail_table,
        tail_state.reshape(1, D), head_rows, tail_rows, negatives, relation_ids,
        block_counts.reshape(2),
    )
    square = pltpu.VMEM((D, D), BF16)
    big = pltpu.VMEM((2, 4, 2, 4, 16, D), BF16)
    scratch = [
        pltpu.VMEM((4, D), F32),
        pltpu.VMEM((4, D), F32),
        pltpu.VMEM((D, D), F32),
        pltpu.VMEM((1, D), F32),
        pltpu.VMEM((D, D), F32),
        pltpu.VMEM((1, D), F32),
        pltpu.VMEM((2, D), I32),
        pltpu.VMEM((2, D), I32),
        pltpu.VMEM((2, EB, BLOCK), I32),
        pltpu.SMEM((2, EB), I32),
        pltpu.SMEM((2,), I32),
        pltpu.VMEM((8, D), F32),
        pltpu.VMEM((8, D), F32),
        pltpu.VMEM((2, 8, D), F32),
        pltpu.VMEM((2, 4, 8, D), F32),
        pltpu.VMEM((16, D), F32),
        pltpu.VMEM((16, D), F32),
        big, big, big, big,
        square, square, square, square, square, square,
        pltpu.VMEM((D, 2 * D), BF16),
        pltpu.VMEM((D, BLOCK), BF16),
        square,
        pltpu.VMEM((D, 2 * D), BF16),
        pltpu.VMEM((2 * D, D), BF16),
        square, square,
        pltpu.VMEM((1, D), F32),
        pltpu.VMEM((1, D), F32),
        dma((11,)), dma((2, 3)), dma((2, 3)), dma((2,)), dma((2,)),
    ]
    scratch += RS_BUFS + RS_BUFS
    scratch += [dma(s) for s in AG_SEMS + AG_SEMS + RS_SEMS + RS_SEMS]
    return pl.pallas_call(
        kernel,
        name="rescal",
        out_shape=(table, table, jax.ShapeDtypeStruct((4, D), F32)),
        in_specs=[ANY] * len(args),
        out_specs=[VMEM] * 3,
        scratch_shapes=scratch,
        compiler_params=pltpu.CompilerParams(
            collective_id=1, has_side_effects=True, vmem_limit_bytes=60 << 20
        ),
    )(*args)


def solution(mesh):
    both = ("head", "tail")
    in_specs = (
        P(both, None),
        P(both),
        P(both, None),
        P(both),
        P(both, None),
        P(both, None),
        P(None, both),
        P(None, both),
        P(None, both, None),
        P(None, both),
        P(None, both),
    )
    out_specs = (P(both, None), P(both, None), P(both, None))
    return jax.shard_map(shards, mesh=mesh, in_specs=in_specs, out_specs=out_specs, check_vma=False)
```

```python
import jax
import jax.numpy as jnp
from jax import lax
from jax.experimental import pallas as pl
from jax.experimental.pallas import tpu as pltpu
from jax.sharding import PartitionSpec as P

MESH = pl.DeviceIdType.MESH
RATE_ROWS = 0.2
RATE_RELATIONS = 0.05
EPSILON = 1e-06
D = 512
EB = 4
BLOCK = 128
F32 = jnp.float32
BF16 = jnp.bfloat16
I32 = jnp.int32
VMEM = pl.BlockSpec(memory_space=pltpu.VMEM)
ANY = pl.BlockSpec(memory_space=pltpu.HBM)


class Place:
    def __init__(self):
        hd, tl = lax.axis_index("head"), lax.axis_index("tail")
        self.core, self.y, self.x = hd % 2, (hd // 2) % 4, tl % 4
        self.z = (hd // 8) * 4 + tl // 4
        self.right, self.left = (hd, (tl + 1) % 16), (hd, (tl + 15) % 16)

    def at(self, core=None, y=None, z=None, x=None):
        core = self.core if core is None else core
        y = self.y if y is None else y
        z = self.z if z is None else z
        x = self.x if x is None else x
        return ((z // 4) * 8 + y * 2 + core, (z % 4) * 4 + x)

    def partner(self):
        return self.at(core=1 - self.core)

    def xd(self, d):
        return (self.x + d) % 4

    def yd(self, d):
        return (self.y + d) % 4

    def zd(self, d):
        return (self.z + d) % 8


def signal_peers(w):
    barrier = pltpu.get_barrier_semaphore()
    peers = [w.partner(), w.right, w.left]
    peers += [w.at(x=w.xd(d)) for d in range(1, 4)]
    peers += [w.at(y=w.yd(d)) for d in range(1, 4)]
    peers += [w.at(z=w.zd(d)) for d in range(1, 8)]
    for peer in peers:
        pl.semaphore_signal(barrier, inc=1, device_id=peer, device_id_type=MESH)
    return barrier, len(peers)


def remote(src, dst, ssem, rsem, to):
    return pltpu.make_async_remote_copy(
        src_ref=src, dst_ref=dst, send_sem=ssem, recv_sem=rsem, device_id=to, device_id_type=MESH
    )


def send(src, dst, ssem, rsem, to):
    copy = remote(src, dst, ssem, rsem, to)
    copy.start()
    return copy


NEAR = (1, 7, 2, 6, 3, 5, 4)
FAR = (4, 3, 5, 2, 6, 1, 7)


def gather_tiles(w, rel, sems, segments):
    zs, zr, ys, yr, cs, cr = sems
    late = []

    def tile(z, y, core):
        return rel.at[z // 4, y, core, z % 4]

    def to_core(t):
        send(t, t, cs.at[0], cr.at[0], w.partner())

    def spread(d):
        t = tile(w.zd(8 - d), w.y, w.core)
        for e in (2, 1, 3):
            late.append(send(t, t, ys.at[e - 1, d], yr.at[e - 1, d], w.at(y=w.yd(e))))
        to_core(t)

    def arrive_z(d):
        t = tile(w.zd(8 - d), w.y, w.core)
        remote(t, t, zs.at[d - 1], zr.at[d - 1], w.partner()).wait_recv()
        spread(d)

    def arrive_y(d):
        for e in (1, 3, 2):
            t = tile(w.zd(8 - d), w.yd(4 - e), w.core)
            remote(t, t, ys.at[e - 1, d], yr.at[e - 1, d], w.partner()).wait_recv()
            to_core(t)

    own = tile(w.z, w.y, w.core)
    for d in FAR:
        late.append(send(own, own, zs.at[d - 1], zr.at[d - 1], w.at(z=w.zd(d))))
    spread(0)
    segments[0]()
    for d in (1, 7, 2, 6):
        arrive_z(d)
    arrive_y(0)
    arrive_z(3)
    arrive_z(5)
    arrive_z(4)
    segments[1]()
    for d in NEAR:
        arrive_y(d)
    other = rel.at[:, :, 1 - w.core]
    half = rel.at[:, :, w.core]
    remote(other, other, cs.at[0], cr.at[0], w.partner()).wait_recv()
    remote(half, half, cs.at[0], cr.at[0], w.partner()).wait_send()
    for copy in late:
        copy.wait_send()


AG_SEMS = [(7,), (7,), (3, 8), (3, 8), (1,), (1,)]


def reduce_tiles(w, g, bufs, sems, segments):
    cbuf, psrc, ybuf, acc, zsrc, zbuf, xt = bufs
    cs, cr, ys, yr, zs, zr, xs, xr = sems
    late = []
    order = FAR + (0,)
    for d in order:
        z = w.zd(d)
        late.append(
            send(g.at[z // 4, :, 1 - w.core, z % 4], cbuf.at[d], cs.at[d], cr.at[d], w.partner())
        )
    for d in order:
        z = w.zd(d)
        remote(cbuf.at[d], cbuf.at[d], cs.at[d], cr.at[d], w.partner()).wait_recv()
        for e in (2, 1, 3):
            y = w.yd(e)
            both = g[z // 4, y, w.core, z % 4].astype(F32) + cbuf[d, y].astype(F32)
            psrc[e - 1, d] = both.astype(BF16)
            late.append(
                send(psrc.at[e - 1, d], ybuf.at[e - 1, d], ys.at[e - 1, d], yr.at[e - 1, d], w.at(y=y))
            )
        acc[d] = g[z // 4, w.y, w.core, z % 4].astype(F32) + cbuf[d, w.y].astype(F32)
    segments[0]()
    total = None
    for d in order:
        total = acc[d]
        for e in (1, 3, 2):
            remote(
                ybuf.at[e - 1, d], ybuf.at[e - 1, d], ys.at[e - 1, d], yr.at[e - 1, d], w.partner()
            ).wait_recv()
            total = total + ybuf[e - 1, d].astype(F32)
        if d > 0:
            zsrc[d - 1] = total.astype(BF16)
            late.append(
                send(zsrc.at[d - 1], zbuf.at[d - 1], zs.at[d - 1], zr.at[d - 1], w.at(z=w.zd(d)))
            )
    acc[0] = total
    segments[1]()
    total = acc[0]
    for d in NEAR:
        remote(
            zbuf.at[d - 1], zbuf.at[d - 1], zs.at[d - 1], zr.at[d - 1], w.partner()
        ).wait_recv()
        total = total + zbuf[d - 1].astype(F32)
    xt[w.x] = total.astype(BF16)
    for e in (2, 1, 3):
        late.append(
            send(xt.at[w.x], xt.at[w.x], xs.at[e - 1], xr.at[e - 1], w.at(x=w.xd(e)))
        )
    segments[2]()
    for e in (1, 3, 2):
        t = xt.at[w.xd(4 - e)]
        remote(t, t, xs.at[e - 1], xr.at[e - 1], w.partner()).wait_recv()
    total = xt[0].astype(F32) + xt[1].astype(F32) + xt[2].astype(F32) + xt[3].astype(F32)
    return total, late


RS_SEMS = [(8,), (8,), (3, 8), (3, 8), (7,), (7,), (3,), (3,)]
RS_BUFS = [
    pltpu.VMEM((8, 4, 16, D), BF16),
    pltpu.VMEM((3, 8, 16, D), BF16),
    pltpu.VMEM((3, 8, 16, D), BF16),
    pltpu.VMEM((8, 16, D), F32),
    pltpu.VMEM((7, 16, D), BF16),
    pltpu.VMEM((7, 16, D), BF16),
    pltpu.VMEM((4, 16, D), BF16),
]


SHIFT_NEAR = (6, 0, 2, 0, 0)
SHIFT_FAR = (2, 0, 4, 0, 2)


def dot(a, b):
    return jnp.dot(a, b, preferred_element_type=F32)


def dot_nt(a, b):
    return lax.dot_general(a, b, (((1,), (1,)), ((), ())), preferred_element_type=F32)


def dot_tn(a, b):
    return lax.dot_general(a, b, (((0,), (0,)), ((), ())), preferred_element_type=F32)


def selectors(idx_row):
    wide = jnp.broadcast_to(idx_row, (BLOCK, BLOCK))
    col = wide.T
    lane = lax.broadcasted_iota(I32, (BLOCK, BLOCK), 1)
    picks = [jnp.where(col == lane + BLOCK * j, 1.0, 0.0) for j in range(4)]
    pick = jnp.concatenate(picks, axis=1).astype(BF16)
    row = lax.broadcasted_iota(I32, (D, BLOCK), 0)
    put = jnp.where(row == jnp.broadcast_to(idx_row, (D, BLOCK)), 1.0, 0.0).astype(BF16)
    return pick, put


def block(b):
    return slice(b * BLOCK, (b + 1) * BLOCK)


def pick_rows(index_of, table, out, put, base):
    for b in range(EB):
        pick, place = selectors(index_of(b))
        out[block(b), :] = dot(pick, table[...]).astype(BF16)
        put[:, base + b * BLOCK : base + (b + 1) * BLOCK] = place


def as_column(row):
    return jnp.broadcast_to(row, (BLOCK, D)).T


def as_row(col):
    return jnp.broadcast_to(col, (D, BLOCK)).T[0:1, :]


def row_update(table, state_row, grad):
    state = as_column(state_row)[:, 0:1] + jnp.mean(grad * grad, axis=1, keepdims=True)
    return table - grad * (RATE_ROWS / (jnp.sqrt(state) + EPSILON)), state


def relation_step(rel, state, grad):
    state = state + grad * grad
    return rel - RATE_RELATIONS * grad / (jnp.sqrt(state) + EPSILON), state


def kernel(
    rel4_in, st4_in, head_in, hstate_in, tail_in, tstate_in,
    hrows_in, trows_in, negs_in, rids_in, counts_in,
    head_out, tail_out, rel_out,
    rel4, st4, head, hstate, tail, tstate, hrows, trows, negs, rids, counts,
    rel8, st8, xsrc, xbuf, rel16, st16, rel_a, rel_b, g_a, g_b,
    hb, tb, h, t, n, u, gu, gn, hput, tput, terms, tnew, tmoved, tsnew, tsmoved,
    load, xsem_s, xsem_r, msem_s, msem_r, *more,
):
    rs_bufs = [more[0:7], more[7:14]]
    more = more[14:]
    ag_sems = [more[0:6], more[6:12]]
    rs_sems = [more[12:20], more[20:28]]
    w = Place()
    barrier, peers = signal_peers(w)
    ins = (rel4_in, st4_in, hrows_in, head_in, rids_in, counts_in, tail_in, trows_in, negs_in,
           hstate_in, tstate_in)
    outs = (rel4, st4, hrows, head, rids, counts, tail, trows, negs, hstate, tstate)
    loads = []
    for i, (a, b) in enumerate(zip(ins, outs)):
        copy = pltpu.make_async_copy(a, b, load.at[i])
        copy.start()
        loads.append(copy)

    def loaded(*which):
        for i in which:
            loads[i].wait()

    def pick_head(k):
        hb[...] = head[...].astype(BF16)
        pick_rows(lambda b: hrows[k : k + 1, block(b)], hb, h, hput, 0)

    def pick_tail(k):
        pick_rows(lambda b: trows[k : k + 1, block(b)], tb, t, tput, 0)

    def pick_negs(k):
        pick_rows(lambda b: negs[k, b : b + 1, :], tb, n, tput, D)

    def score(k, rel, g):
        r0, r1 = rel[0].reshape(D, D), rel[1].reshape(D, D)
        for b in range(EB):
            rows = block(b)
            live = (b < counts[k]).astype(F32)
            one = (rids[k, b] == 1).astype(F32)
            ub = dot(h[rows, :], jnp.where(rids[k, b] == 1, r1, r0)).astype(BF16)
            u[rows, :] = ub
            tf = t[rows, :].astype(F32)
            uf = ub.astype(F32)
            gp = -live * jax.nn.sigmoid(-jnp.sum(uf * tf, axis=1, keepdims=True))
            gnb = (live * jax.nn.sigmoid(dot_nt(ub, n[rows, :])) / BLOCK).astype(BF16)
            gn[rows, :] = gnb
            gub = (gp * tf + dot(gnb, n[rows, :])).astype(BF16).astype(F32)
            gu[rows, 0:D] = (gub * (1.0 - one)).astype(BF16)
            gu[rows, D:] = (gub * one).astype(BF16)
            terms[rows, :] = (gp * uf).astype(BF16)
        g[0] = dot_tn(h[...], gu[:, 0:D]).astype(BF16).reshape(4, 2, 4, 16, D)
        g[1] = dot_tn(h[...], gu[:, D:]).astype(BF16).reshape(4, 2, 4, 16, D)

    def tail_grad():
        for b in range(EB):
            rows = block(b)
            terms[D + b * BLOCK : D + (b + 1) * BLOCK, :] = dot_tn(gn[rows, :], u[rows, :]).astype(BF16)
        return dot(tput[...], terms[...])

    def head_grad(rel):
        r0, r1 = rel[0].reshape(D, D), rel[1].reshape(D, D)
        hterms = dot_nt(gu[:, 0:D], r0) + dot_nt(gu[:, D:], r1)
        return dot(hput[...], hterms.astype(BF16))

    nothing = lambda: None

    loaded(0, 1)
    rel8[0:4, :] = rel4[...]
    rel8[4:8, :] = rel4[...]
    st8[0:4, :] = st4[...]
    st8[4:8, :] = st4[...]
    mine = lax.broadcasted_iota(I32, (8, D), 0) // 4 == w.x % 2
    xsrc[0] = jnp.where(mine, rel8[...], 0.0)
    xsrc[1] = jnp.where(mine, st8[...], 0.0)
    pl.semaphore_wait(barrier, peers)
    xsends = []
    for part in range(2):
        for e in (2, 1, 3):
            xsends.append(
                send(
                    xsrc.at[part], xbuf.at[part, w.x],
                    xsem_s.at[part, e - 1], xsem_r.at[part, e - 1], w.at(x=w.xd(e)),
                )
            )
        xbuf[part, w.x] = xsrc[part]
    loaded(2, 3)
    pick_head(0)
    loaded(6, 7)
    tb[...] = tail[...].astype(BF16)
    pick_tail(0)

    def merge(part, out):
        for e in (1, 3, 2):
            to = xbuf.at[part, w.xd(4 - e)]
            remote(
                to, to, xsem_s.at[part, e - 1], xsem_r.at[part, e - 1], w.partner()
            ).wait_recv()
        out[0:8, :] = xbuf[part, 0] + xbuf[part, 1]
        out[8:16, :] = xbuf[part, 2] + xbuf[part, 3]

    merge(0, rel16)
    rel_a[w.z // 4, w.y, w.core, w.z % 4] = rel16[...].astype(BF16)

    def negs_first():
        loaded(8)
        pick_negs(0)

    gather_tiles(w, rel_a, ag_sems[0], (negs_first, nothing))
    loaded(4, 5, 9, 10)

    score(0, rel_a, g_a)
    sent = {False: 0, True: 0}

    def chunk(c):
        rows = slice(c * 64, (c + 1) * 64)
        return remote(tnew.at[rows], tmoved.at[rows], msem_s.at[c], msem_r.at[c], w.right)

    def shift(point):
        for far, plan in ((False, SHIFT_NEAR), (True, SHIFT_FAR)):
            first, count = sent[far], plan[point]
            sent[far] += count
            if count > 0:

                @pl.when((w.x == 3) == far)
                def _():
                    for c in range(first, first + count):
                        chunk(c).start()

    def tail_step():
        new, state = row_update(tail[...], tstate[...], tail_grad())
        tnew[...] = new.astype(BF16)
        tsnew[...] = as_row(state)
        send(tsnew, tsmoved, msem_s.at[8], msem_r.at[8], w.right)
        shift(0)

    def head_step():
        shift(1)
        new, state = row_update(head[...], hstate[...], head_grad(rel_a))
        head[...] = new
        hstate[...] = as_row(state)

    def head_again():
        shift(2)
        pick_head(1)

    grad, late = reduce_tiles(
        w, g_a, rs_bufs[0], rs_sems[0], (tail_step, head_step, head_again)
    )
    merge(1, st16)
    new, state = relation_step(rel16[...], st16[...], grad)
    rel16[...] = new
    st16[...] = state
    rel_b[w.z // 4, w.y, w.core, w.z % 4] = new.astype(BF16)

    def tail_arrives():
        shift(4)
        for c in range(8):
            chunk(c).wait()
        remote(tsnew, tsmoved, msem_s.at[8], msem_r.at[8], w.right).wait()
        pick_rows(lambda b: trows[1:2, block(b)], tmoved, t, tput, 0)
        pick_rows(lambda b: negs[1, b : b + 1, :], tmoved, n, tput, D)

    gather_tiles(
        w, rel_b, ag_sems[1],
        (lambda: shift(3), tail_arrives),
    )

    score(1, rel_b, g_b)

    def tail_last():
        new, _ = row_update(tmoved[...].astype(F32), tsmoved[...], tail_grad())
        tail_out[...] = new

    def head_last():
        new, _ = row_update(head[...], hstate[...], head_grad(rel_b))
        head_out[...] = new

    grad, later = reduce_tiles(
        w, g_b, rs_bufs[1], rs_sems[1], (tail_last, head_last, nothing)
    )
    new, _ = relation_step(rel16[...], st16[...], grad)
    out = new[0:4]
    for i in range(1, 4):
        out = jnp.where(w.x == i, new[4 * i : 4 * i + 4], out)
    rel_out[...] = out
    for copy in xsends + late + later:
        copy.wait_send()


def dma(shape):
    return pltpu.SemaphoreType.DMA(shape)


def shards(
    head_table,
    head_state,
    tail_table,
    tail_state,
    relations,
    relation_state,
    head_rows,
    tail_rows,
    negatives,
    relation_ids,
    block_counts,
):
    table = jax.ShapeDtypeStruct((D, D), F32)
    args = (
        relations, relation_state, head_table, head_state.reshape(1, D), tail_table,
        tail_state.reshape(1, D), head_rows, tail_rows, negatives, relation_ids,
        block_counts.reshape(2),
    )
    args = tuple(pltpu.with_memory_space_constraint(a, pltpu.HBM) for a in args)
    square = pltpu.VMEM((D, D), BF16)
    big = pltpu.VMEM((2, 4, 2, 4, 16, D), BF16)
    scratch = [
        pltpu.VMEM((4, D), F32),
        pltpu.VMEM((4, D), F32),
        pltpu.VMEM((D, D), F32),
        pltpu.VMEM((1, D), F32),
        pltpu.VMEM((D, D), F32),
        pltpu.VMEM((1, D), F32),
        pltpu.VMEM((2, D), I32),
        pltpu.VMEM((2, D), I32),
        pltpu.VMEM((2, EB, BLOCK), I32),
        pltpu.SMEM((2, EB), I32),
        pltpu.SMEM((2,), I32),
        pltpu.VMEM((8, D), F32),
        pltpu.VMEM((8, D), F32),
        pltpu.VMEM((2, 8, D), F32),
        pltpu.VMEM((2, 4, 8, D), F32),
        pltpu.VMEM((16, D), F32),
        pltpu.VMEM((16, D), F32),
        big, big, big, big,
        square, square, square, square, square, square,
        pltpu.VMEM((D, 2 * D), BF16),
        pltpu.VMEM((D, BLOCK), BF16),
        square,
        pltpu.VMEM((D, 2 * D), BF16),
        pltpu.VMEM((2 * D, D), BF16),
        square, square,
        pltpu.VMEM((1, D), F32),
        pltpu.VMEM((1, D), F32),
        dma((11,)), dma((2, 3)), dma((2, 3)), dma((9,)), dma((9,)),
    ]
    scratch += RS_BUFS + RS_BUFS
    scratch += [dma(s) for s in AG_SEMS + AG_SEMS + RS_SEMS + RS_SEMS]
    return pl.pallas_call(
        kernel,
        name="rescal",
        out_shape=(table, table, jax.ShapeDtypeStruct((4, D), F32)),
        in_specs=[ANY] * len(args),
        out_specs=[VMEM] * 3,
        scratch_shapes=scratch,
        compiler_params=pltpu.CompilerParams(
            collective_id=1, has_side_effects=True, vmem_limit_bytes=30 << 20
        ),
    )(*args)


def solution(mesh):
    both = ("head", "tail")
    in_specs = (
        P(both, None),
        P(both),
        P(both, None),
        P(both),
        P(both, None),
        P(both, None),
        P(None, both),
        P(None, both),
        P(None, both, None),
        P(None, both),
        P(None, both),
    )
    out_specs = (P(both, None), P(both, None), P(both, None))
    return jax.shard_map(shards, mesh=mesh, in_specs=in_specs, out_specs=out_specs, check_vma=False)
```

```python
import jax
import jax.numpy as jnp
from jax import lax
from jax.experimental import pallas as pl
from jax.experimental.pallas import tpu as pltpu
from jax.sharding import PartitionSpec as P

MESH = pl.DeviceIdType.MESH
RATE_ROWS = 0.2
RATE_RELATIONS = 0.05
EPSILON = 1e-06
D = 512
EB = 4
BLOCK = 128
F32 = jnp.float32
BF16 = jnp.bfloat16
I32 = jnp.int32
VMEM = pl.BlockSpec(memory_space=pltpu.VMEM)
ANY = pl.BlockSpec(memory_space=pltpu.HBM)


class Place:
    def __init__(self):
        hd, tl = lax.axis_index("head"), lax.axis_index("tail")
        self.core, self.y, self.x = hd % 2, (hd // 2) % 4, tl % 4
        self.z = (hd // 8) * 4 + tl // 4
        self.right, self.left = (hd, (tl + 1) % 16), (hd, (tl + 15) % 16)
        self.row = [(hd, tl - self.x + r) for r in range(4)]
        self.next_first = (hd, (tl - self.x + 4) % 16)
        self.row_before = [(hd, (tl - self.x + 12 + r) % 16) for r in range(4)]

    def at(self, core=None, y=None, z=None, x=None):
        core = self.core if core is None else core
        y = self.y if y is None else y
        z = self.z if z is None else z
        x = self.x if x is None else x
        return ((z // 4) * 8 + y * 2 + core, (z % 4) * 4 + x)

    def partner(self):
        return self.at(core=1 - self.core)

    def xd(self, d):
        return (self.x + d) % 4

    def yd(self, d):
        return (self.y + d) % 4

    def zd(self, d):
        return (self.z + d) % 8


NEAR = (1, 7, 2, 6, 3, 5, 4)
FAR = (4, 3, 5, 2, 6, 1, 7)


def signal_peers(w):
    barrier = pltpu.get_barrier_semaphore()
    peers = [w.at(z=w.zd(d)) for d in FAR] + [w.right, w.left]
    peers += [w.at(y=w.yd(d)) for d in (2, 1, 3)] + [w.at(x=w.xd(d)) for d in (2, 1, 3)]
    peers.append(w.partner())
    for peer in peers:
        pl.semaphore_signal(barrier, inc=1, device_id=peer, device_id_type=MESH)

    @pl.when(w.x == 0)
    def _():
        for r in (1, 2):
            pl.semaphore_signal(
                barrier, inc=1, device_id=w.row_before[r], device_id_type=MESH
            )

    @pl.when((w.x == 1) | (w.x == 2))
    def _():
        pl.semaphore_signal(barrier, inc=1, device_id=w.next_first, device_id_type=MESH)

    extra = jnp.where(w.x == 0, 2, jnp.where(w.x == 3, 0, 1))
    return barrier, len(peers) + extra


def remote(src, dst, ssem, rsem, to):
    return pltpu.make_async_remote_copy(
        src_ref=src, dst_ref=dst, send_sem=ssem, recv_sem=rsem, device_id=to, device_id_type=MESH
    )


def send(src, dst, ssem, rsem, to):
    copy = remote(src, dst, ssem, rsem, to)
    copy.start()
    return copy


def gather_tiles(w, rel, sems, segments):
    zs, zr, ys, yr, cs, cr = sems
    late = []

    def tile(z, y, core):
        return rel.at[z // 4, y, core, z % 4]

    def to_core(t):
        send(t, t, cs.at[0], cr.at[0], w.partner())

    def spread(d):
        t = tile(w.zd(8 - d), w.y, w.core)
        for e in (2, 1, 3):
            late.append(send(t, t, ys.at[e - 1, d], yr.at[e - 1, d], w.at(y=w.yd(e))))
        to_core(t)

    def arrive_z(d):
        t = tile(w.zd(8 - d), w.y, w.core)
        remote(t, t, zs.at[d - 1], zr.at[d - 1], w.partner()).wait_recv()
        spread(d)

    def arrive_y(d):
        for e in (1, 3, 2):
            t = tile(w.zd(8 - d), w.yd(4 - e), w.core)
            remote(t, t, ys.at[e - 1, d], yr.at[e - 1, d], w.partner()).wait_recv()
            to_core(t)

    own = tile(w.z, w.y, w.core)
    for d in FAR:
        late.append(send(own, own, zs.at[d - 1], zr.at[d - 1], w.at(z=w.zd(d))))
    spread(0)
    segments[0]()
    for d in (1, 7, 2, 6):
        arrive_z(d)
    segments[2]()
    arrive_y(0)
    arrive_z(3)
    arrive_z(5)
    arrive_z(4)
    segments[1]()
    for d in NEAR:
        arrive_y(d)
    other = rel.at[:, :, 1 - w.core]
    half = rel.at[:, :, w.core]
    remote(other, other, cs.at[0], cr.at[0], w.partner()).wait_recv()
    remote(half, half, cs.at[0], cr.at[0], w.partner()).wait_send()
    for copy in late:
        copy.wait_send()


AG_SEMS = [(7,), (7,), (3, 8), (3, 8), (1,), (1,)]


def reduce_tiles(w, g, bufs, sems, segments):
    cbuf, psrc, ybuf, acc, zsrc, zbuf, xt = bufs
    cs, cr, ys, yr, zs, zr, xs, xr = sems
    late = []
    order = FAR + (0,)
    for d in order:
        z = w.zd(d)
        late.append(
            send(g.at[z // 4, :, 1 - w.core, z % 4], cbuf.at[d], cs.at[d], cr.at[d], w.partner())
        )
    for d in order:
        z = w.zd(d)
        remote(cbuf.at[d], cbuf.at[d], cs.at[d], cr.at[d], w.partner()).wait_recv()
        for e in (2, 1, 3):
            y = w.yd(e)
            both = g[z // 4, y, w.core, z % 4].astype(F32) + cbuf[d, y].astype(F32)
            psrc[e - 1, d] = both.astype(BF16)
            late.append(
                send(psrc.at[e - 1, d], ybuf.at[e - 1, d], ys.at[e - 1, d], yr.at[e - 1, d], w.at(y=y))
            )
        acc[d] = g[z // 4, w.y, w.core, z % 4].astype(F32) + cbuf[d, w.y].astype(F32)
    segments[0]()
    total = None
    for d in order:
        total = acc[d]
        for e in (1, 3, 2):
            remote(
                ybuf.at[e - 1, d], ybuf.at[e - 1, d], ys.at[e - 1, d], yr.at[e - 1, d], w.partner()
            ).wait_recv()
            total = total + ybuf[e - 1, d].astype(F32)
        if d > 0:
            zsrc[d - 1] = total.astype(BF16)
            late.append(
                send(zsrc.at[d - 1], zbuf.at[d - 1], zs.at[d - 1], zr.at[d - 1], w.at(z=w.zd(d)))
            )
    acc[0] = total
    segments[1]()
    total = acc[0]
    for d in NEAR:
        remote(
            zbuf.at[d - 1], zbuf.at[d - 1], zs.at[d - 1], zr.at[d - 1], w.partner()
        ).wait_recv()
        total = total + zbuf[d - 1].astype(F32)
    xt[w.x] = total.astype(BF16)
    for e in (2, 1, 3):
        late.append(
            send(xt.at[w.x], xt.at[w.x], xs.at[e - 1], xr.at[e - 1], w.at(x=w.xd(e)))
        )
    segments[2]()
    for e in (1, 3, 2):
        t = xt.at[w.xd(4 - e)]
        remote(t, t, xs.at[e - 1], xr.at[e - 1], w.partner()).wait_recv()
    total = xt[0].astype(F32) + xt[1].astype(F32) + xt[2].astype(F32) + xt[3].astype(F32)
    return total, late


RS_SEMS = [(8,), (8,), (3, 8), (3, 8), (7,), (7,), (3,), (3,)]
RS_BUFS = [
    pltpu.VMEM((8, 4, 16, D), BF16),
    pltpu.VMEM((3, 8, 16, D), BF16),
    pltpu.VMEM((3, 8, 16, D), BF16),
    pltpu.VMEM((8, 16, D), F32),
    pltpu.VMEM((7, 16, D), BF16),
    pltpu.VMEM((7, 16, D), BF16),
    pltpu.VMEM((4, 16, D), BF16),
]


SHIFT = (6, 2)


def dot(a, b):
    return jnp.dot(a, b, preferred_element_type=F32)


def dot_nt(a, b):
    return lax.dot_general(a, b, (((1,), (1,)), ((), ())), preferred_element_type=F32)


def dot_tn(a, b):
    return lax.dot_general(a, b, (((0,), (0,)), ((), ())), preferred_element_type=F32)


def selectors(idx_row):
    wide = jnp.broadcast_to(idx_row, (BLOCK, BLOCK))
    col = wide.T
    lane = lax.broadcasted_iota(I32, (BLOCK, BLOCK), 1)
    picks = [jnp.where(col == lane + BLOCK * j, 1.0, 0.0) for j in range(4)]
    pick = jnp.concatenate(picks, axis=1).astype(BF16)
    row = lax.broadcasted_iota(I32, (D, BLOCK), 0)
    put = jnp.where(row == jnp.broadcast_to(idx_row, (D, BLOCK)), 1.0, 0.0).astype(BF16)
    return pick, put


def block(b):
    return slice(b * BLOCK, (b + 1) * BLOCK)


def pick_rows(index_of, table, out, put, base):
    for b in range(EB):
        pick, place = selectors(index_of(b))
        out[block(b), :] = dot(pick, table[...]).astype(BF16)
        put[:, base + b * BLOCK : base + (b + 1) * BLOCK] = place


def as_column(row):
    return jnp.broadcast_to(row, (BLOCK, D)).T


def as_row(col):
    return jnp.broadcast_to(col, (D, BLOCK)).T[0:1, :]


def row_update(table, state_row, grad):
    state = as_column(state_row)[:, 0:1] + jnp.mean(grad * grad, axis=1, keepdims=True)
    return table - grad * (RATE_ROWS / (jnp.sqrt(state) + EPSILON)), state


def relation_step(rel, state, grad):
    state = state + grad * grad
    return rel - RATE_RELATIONS * grad / (jnp.sqrt(state) + EPSILON), state


def kernel(
    rel4_in, st4_in, head_in, hstate_in, tail_in, tstate_in,
    hrows_in, trows_in, negs_in, rids_in, counts_in,
    head_out, tail_out, rel_out,
    rel4, st4, head, hstate, tail, tstate, hrows, trows, negs, rids, counts,
    rel8, st8, xsrc, xbuf, rel16, st16, rel_a, rel_b, g_a, g_b,
    hb, tb, h, ht, t, n, u, gu, gn, hput, tput, terms, tnew, tmoved, tsnew, tsmoved,
    load, xsem_s, xsem_r, msem_s, msem_r, hop, hop_s, hop_r, *more,
):
    rs_bufs = [more[0:7], more[7:14]]
    more = more[14:]
    ag_sems = [more[0:6], more[6:12]]
    rs_sems = [more[12:20], more[20:28]]
    w = Place()
    barrier, peers = signal_peers(w)
    ins = (rel4_in, st4_in, hrows_in, head_in, rids_in, counts_in, tail_in, trows_in, negs_in,
           hstate_in, tstate_in)
    outs = (rel4, st4, hrows, head, rids, counts, tail, trows, negs, hstate, tstate)
    loads = []
    for i, (a, b) in enumerate(zip(ins, outs)):
        copy = pltpu.make_async_copy(a, b, load.at[i])
        copy.start()
        loads.append(copy)

    def loaded(*which):
        for i in which:
            loads[i].wait()

    def pick_head(k):
        hb[...] = head[...].astype(BF16)
        pick_rows(lambda b: hrows[k : k + 1, block(b)], hb, h, hput, 0)
        ht[...] = dot_tn(hb[...], hput[...]).astype(BF16)

    def pick_tail(k):
        pick_rows(lambda b: trows[k : k + 1, block(b)], tb, t, tput, 0)

    def pick_negs(k):
        pick_rows(lambda b: negs[k, b : b + 1, :], tb, n, tput, D)

    def score(k, rel, g):
        r0, r1 = rel[0].reshape(D, D), rel[1].reshape(D, D)
        ub, gp, gnb = [], [], []
        for b in range(EB):
            chosen = jnp.where(rids[k, b] == 1, r1, r0)
            ub.append(dot(h[block(b), :], chosen).astype(BF16))
        neg = [dot_nt(ub[b], n[block(b), :]) for b in range(EB)]
        for b in range(EB):
            u[block(b), :] = ub[b]
            live = (b < counts[k]).astype(F32)
            gnb.append((live * jax.nn.sigmoid(neg[b]) / BLOCK).astype(BF16))
            gn[block(b), :] = gnb[b]
            pos = jnp.sum(
                ub[b].astype(F32) * t[block(b), :].astype(F32), axis=1, keepdims=True
            )
            gp.append(-live * jax.nn.sigmoid(-pos))
        back = [dot(gnb[b], n[block(b), :]) for b in range(EB)]
        for b in range(EB):
            one = (rids[k, b] == 1).astype(F32)
            gub = (gp[b] * t[block(b), :].astype(F32) + back[b]).astype(BF16).astype(F32)
            gu[block(b), 0:D] = (gub * (1.0 - one)).astype(BF16)
            gu[block(b), D:] = (gub * one).astype(BF16)
        g[0] = dot(ht[...], gu[:, 0:D]).astype(BF16).reshape(4, 2, 4, 16, D)
        g[1] = dot(ht[...], gu[:, D:]).astype(BF16).reshape(4, 2, 4, 16, D)
        for b in range(EB):
            terms[block(b), :] = (gp[b] * ub[b].astype(F32)).astype(BF16)

    def tail_grad():
        for b in range(EB):
            rows = block(b)
            terms[D + b * BLOCK : D + (b + 1) * BLOCK, :] = dot_tn(gn[rows, :], u[rows, :]).astype(BF16)
        return dot(tput[...], terms[...])

    def head_grad(rel):
        r0, r1 = rel[0].reshape(D, D), rel[1].reshape(D, D)
        hterms = dot_nt(gu[:, 0:D], r0) + dot_nt(gu[:, D:], r1)
        return dot(hput[...], hterms.astype(BF16))

    nothing = lambda: None

    loaded(0, 1)
    rel8[0:4, :] = rel4[...]
    rel8[4:8, :] = rel4[...]
    st8[0:4, :] = st4[...]
    st8[4:8, :] = st4[...]
    mine = lax.broadcasted_iota(I32, (8, D), 0) // 4 == w.x % 2
    xsrc[0] = jnp.where(mine, rel8[...], 0.0)
    xsrc[1] = jnp.where(mine, st8[...], 0.0)
    pl.semaphore_wait(barrier, peers)
    xsends = []
    for part in range(2):
        for e in (2, 1, 3):
            xsends.append(
                send(
                    xsrc.at[part], xbuf.at[part, w.x],
                    xsem_s.at[part, e - 1], xsem_r.at[part, e - 1], w.at(x=w.xd(e)),
                )
            )
        xbuf[part, w.x] = xsrc[part]
    loaded(2, 3)
    pick_head(0)
    loaded(6, 7)
    tb[...] = tail[...].astype(BF16)
    pick_tail(0)

    def merge(part, out):
        for e in (1, 3, 2):
            to = xbuf.at[part, w.xd(4 - e)]
            remote(
                to, to, xsem_s.at[part, e - 1], xsem_r.at[part, e - 1], w.partner()
            ).wait_recv()
        out[0:8, :] = xbuf[part, 0] + xbuf[part, 1]
        out[8:16, :] = xbuf[part, 2] + xbuf[part, 3]

    merge(0, rel16)
    rel_a[w.z // 4, w.y, w.core, w.z % 4] = rel16[...].astype(BF16)

    def negs_first():
        loaded(8)
        pick_negs(0)

    gather_tiles(w, rel_a, ag_sems[0], (negs_first, nothing, nothing))
    loaded(4, 5, 9, 10)

    score(0, rel_a, g_a)
    def rows_of(c):
        return pl.ds(pl.multiple_of(c * 64, 64), 64)

    def chunk(c):
        part = slice(c * 64, (c + 1) * 64)
        return remote(tnew.at[part], tmoved.at[part], msem_s.at[c], msem_r.at[c], w.right)

    def shift(first, last):
        @pl.when(w.x < 3)
        def _():
            for c in range(first, last):
                chunk(c).start()

    def shift_far():
        @pl.when(w.x == 3)
        def _():
            for c in (0, 1, 2, 4, 5, 6):
                part = slice(c * 64, (c + 1) * 64)
                remote(
                    tnew.at[part], hop.at[c // 4], msem_s.at[c], hop_r.at[c // 4], w.row[c % 4]
                ).start()

    def relayed(i):
        c = w.x + 4 * i
        return remote(hop.at[i], tmoved.at[rows_of(c)], hop_s.at[i], msem_r.at[c], w.next_first)

    def relay(which):
        @pl.when(w.x == 3)
        def _():
            for i in which:
                chunk(3 + 4 * i).start()

        @pl.when(w.x < 3)
        def _():
            for i in which:
                remote(hop.at[i], hop.at[i], hop_s.at[i], hop_r.at[i], w.right).wait_recv()
                relayed(i).start()

    def tail_step():
        new, state = row_update(tail[...], tstate[...], tail_grad())
        tnew[...] = new.astype(BF16)
        tsnew[...] = as_row(state)
        send(tsnew, tsmoved, msem_s.at[8], msem_r.at[8], w.right)
        shift_far()
        shift(0, SHIFT[0])

    def head_step():
        new, state = row_update(head[...], hstate[...], head_grad(rel_a))
        head[...] = new
        hstate[...] = as_row(state)

    def head_again():
        shift(SHIFT[0], 8)
        pick_head(1)

    grad, late = reduce_tiles(
        w, g_a, rs_bufs[0], rs_sems[0], (tail_step, head_step, head_again)
    )
    merge(1, st16)
    new, state = relation_step(rel16[...], st16[...], grad)
    rel16[...] = new
    st16[...] = state
    rel_b[w.z // 4, w.y, w.core, w.z % 4] = new.astype(BF16)

    def tail_arrives():
        for c in range(8):
            chunk(c).wait()

        @pl.when(w.x < 3)
        def _():
            for i in range(2):
                relayed(i).wait_send()

        remote(tsnew, tsmoved, msem_s.at[8], msem_r.at[8], w.right).wait()
        pick_rows(lambda b: trows[1:2, block(b)], tmoved, t, tput, 0)
        pick_rows(lambda b: negs[1, b : b + 1, :], tmoved, n, tput, D)

    gather_tiles(
        w, rel_b, ag_sems[1],
        (lambda: relay((0, 1)), tail_arrives, nothing),
    )

    score(1, rel_b, g_b)

    def tail_last():
        new, _ = row_update(tmoved[...].astype(F32), tsmoved[...], tail_grad())
        tail_out[...] = new

    def head_last():
        new, _ = row_update(head[...], hstate[...], head_grad(rel_b))
        head_out[...] = new

    grad, later = reduce_tiles(
        w, g_b, rs_bufs[1], rs_sems[1], (tail_last, head_last, nothing)
    )
    new, _ = relation_step(rel16[...], st16[...], grad)
    out = new[0:4]
    for i in range(1, 4):
        out = jnp.where(w.x == i, new[4 * i : 4 * i + 4], out)
    rel_out[...] = out
    for copy in xsends + late + later:
        copy.wait_send()


def dma(shape):
    return pltpu.SemaphoreType.DMA(shape)


def shards(
    head_table,
    head_state,
    tail_table,
    tail_state,
    relations,
    relation_state,
    head_rows,
    tail_rows,
    negatives,
    relation_ids,
    block_counts,
):
    table = jax.ShapeDtypeStruct((D, D), F32)
    args = (
        relations, relation_state, head_table, head_state.reshape(1, D), tail_table,
        tail_state.reshape(1, D), head_rows, tail_rows, negatives, relation_ids,
        block_counts.reshape(2),
    )
    args = tuple(pltpu.with_memory_space_constraint(a, pltpu.HBM) for a in args)
    square = pltpu.VMEM((D, D), BF16)
    big = pltpu.VMEM((2, 4, 2, 4, 16, D), BF16)
    scratch = [
        pltpu.VMEM((4, D), F32),
        pltpu.VMEM((4, D), F32),
        pltpu.VMEM((D, D), F32),
        pltpu.VMEM((1, D), F32),
        pltpu.VMEM((D, D), F32),
        pltpu.VMEM((1, D), F32),
        pltpu.VMEM((2, D), I32),
        pltpu.VMEM((2, D), I32),
        pltpu.VMEM((2, EB, BLOCK), I32),
        pltpu.SMEM((2, EB), I32),
        pltpu.SMEM((2,), I32),
        pltpu.VMEM((8, D), F32),
        pltpu.VMEM((8, D), F32),
        pltpu.VMEM((2, 8, D), F32),
        pltpu.VMEM((2, 4, 8, D), F32),
        pltpu.VMEM((16, D), F32),
        pltpu.VMEM((16, D), F32),
        big, big, big, big,
        square, square, square, square, square, square, square,
        pltpu.VMEM((D, 2 * D), BF16),
        pltpu.VMEM((D, BLOCK), BF16),
        square,
        pltpu.VMEM((D, 2 * D), BF16),
        pltpu.VMEM((2 * D, D), BF16),
        square, square,
        pltpu.VMEM((1, D), F32),
        pltpu.VMEM((1, D), F32),
        dma((11,)), dma((2, 3)), dma((2, 3)), dma((9,)), dma((9,)),
        pltpu.VMEM((2, 64, D), BF16), dma((2,)), dma((2,)),
    ]
    scratch += RS_BUFS + RS_BUFS
    scratch += [dma(s) for s in AG_SEMS + AG_SEMS + RS_SEMS + RS_SEMS]
    return pl.pallas_call(
        kernel,
        name="rescal",
        out_shape=(table, table, jax.ShapeDtypeStruct((4, D), F32)),
        in_specs=[ANY] * len(args),
        out_specs=[VMEM] * 3,
        scratch_shapes=scratch,
        compiler_params=pltpu.CompilerParams(
            collective_id=1, has_side_effects=True, vmem_limit_bytes=30 << 20
        ),
    )(*args)


def solution(mesh):
    both = ("head", "tail")
    in_specs = (
        P(both, None),
        P(both),
        P(both, None),
        P(both),
        P(both, None),
        P(both, None),
        P(None, both),
        P(None, both),
        P(None, both, None),
        P(None, both),
        P(None, both),
    )
    out_specs = (P(both, None), P(both, None), P(both, None))
    return jax.shard_map(shards, mesh=mesh, in_specs=in_specs, out_specs=out_specs, check_vma=False)
```

```python
import jax
import jax.numpy as jnp
from jax import lax
from jax.experimental import pallas as pl
from jax.experimental.pallas import tpu as pltpu
from jax.sharding import PartitionSpec as P

MESH = pl.DeviceIdType.MESH
RATE_ROWS = 0.2
RATE_RELATIONS = 0.05
EPSILON = 1e-06
D = 512
EB = 4
BLOCK = 128
F32 = jnp.float32
BF16 = jnp.bfloat16
I32 = jnp.int32
VMEM = pl.BlockSpec(memory_space=pltpu.VMEM)
ANY = pl.BlockSpec(memory_space=pltpu.HBM)


class Place:
    def __init__(self):
        hd, tl = lax.axis_index("head"), lax.axis_index("tail")
        self.core, self.y, self.x = hd % 2, (hd // 2) % 4, tl % 4
        self.z = (hd // 8) * 4 + tl // 4
        self.right, self.left = (hd, (tl + 1) % 16), (hd, (tl + 15) % 16)
        self.row = [(hd, tl - self.x + r) for r in range(4)]
        self.next_first = (hd, (tl - self.x + 4) % 16)
        self.row_before = [(hd, (tl - self.x + 12 + r) % 16) for r in range(4)]

    def at(self, core=None, y=None, z=None, x=None):
        core = self.core if core is None else core
        y = self.y if y is None else y
        z = self.z if z is None else z
        x = self.x if x is None else x
        return ((z // 4) * 8 + y * 2 + core, (z % 4) * 4 + x)

    def partner(self):
        return self.at(core=1 - self.core)

    def xd(self, d):
        return (self.x + d) % 4

    def yd(self, d):
        return (self.y + d) % 4

    def zd(self, d):
        return (self.z + d) % 8


NEAR = (1, 7, 2, 6, 3, 5, 4)
FAR = (4, 3, 5, 2, 6, 1, 7)


def signal_peers(w):
    barrier = pltpu.get_barrier_semaphore()
    peers = [w.at(z=w.zd(d)) for d in FAR] + [w.right, w.left]
    peers += [w.at(y=w.yd(d)) for d in (2, 1, 3)] + [w.at(x=w.xd(d)) for d in (2, 1, 3)]
    peers.append(w.partner())
    for peer in peers:
        pl.semaphore_signal(barrier, inc=1, device_id=peer, device_id_type=MESH)

    @pl.when(w.x == 0)
    def _():
        for r in (1, 2):
            pl.semaphore_signal(
                barrier, inc=1, device_id=w.row_before[r], device_id_type=MESH
            )

    @pl.when((w.x == 1) | (w.x == 2))
    def _():
        pl.semaphore_signal(barrier, inc=1, device_id=w.next_first, device_id_type=MESH)

    extra = jnp.where(w.x == 0, 2, jnp.where(w.x == 3, 0, 1))
    return barrier, len(peers) + extra


def remote(src, dst, ssem, rsem, to):
    return pltpu.make_async_remote_copy(
        src_ref=src, dst_ref=dst, send_sem=ssem, recv_sem=rsem, device_id=to, device_id_type=MESH
    )


def send(src, dst, ssem, rsem, to):
    copy = remote(src, dst, ssem, rsem, to)
    copy.start()
    return copy


def gather_tiles(w, rel, sems, segments):
    zs, zr, ys, yr, cs, cr = sems
    late = []

    def tile(z, y, core):
        return rel.at[z // 4, y, core, z % 4]

    def to_core(t):
        send(t, t, cs.at[0], cr.at[0], w.partner())

    def spread(d):
        t = tile(w.zd(8 - d), w.y, w.core)
        for e in (2, 1, 3):
            late.append(send(t, t, ys.at[e - 1, d], yr.at[e - 1, d], w.at(y=w.yd(e))))
        to_core(t)

    def arrive_z(d):
        t = tile(w.zd(8 - d), w.y, w.core)
        remote(t, t, zs.at[d - 1], zr.at[d - 1], w.partner()).wait_recv()
        spread(d)

    def arrive_y(d):
        for e in (1, 3, 2):
            t = tile(w.zd(8 - d), w.yd(4 - e), w.core)
            remote(t, t, ys.at[e - 1, d], yr.at[e - 1, d], w.partner()).wait_recv()
            to_core(t)

    own = tile(w.z, w.y, w.core)
    for d in FAR:
        late.append(send(own, own, zs.at[d - 1], zr.at[d - 1], w.at(z=w.zd(d))))
    spread(0)
    segments[0]()
    for d in (1, 7, 2, 6):
        arrive_z(d)
    segments[2]()
    arrive_y(0)
    arrive_z(3)
    arrive_z(5)
    arrive_z(4)
    segments[1]()
    for d in NEAR:
        arrive_y(d)
    other = rel.at[:, :, 1 - w.core]
    half = rel.at[:, :, w.core]
    remote(other, other, cs.at[0], cr.at[0], w.partner()).wait_recv()
    remote(half, half, cs.at[0], cr.at[0], w.partner()).wait_send()
    for copy in late:
        copy.wait_send()


AG_SEMS = [(7,), (7,), (3, 8), (3, 8), (1,), (1,)]


def reduce_tiles(w, g, bufs, sems, segments):
    cbuf, psrc, ybuf, acc, zsrc, zbuf, xt = bufs
    cs, cr, ys, yr, zs, zr, xs, xr = sems
    late = []
    order = FAR + (0,)
    for d in order:
        z = w.zd(d)
        late.append(
            send(g.at[z // 4, :, 1 - w.core, z % 4], cbuf.at[d], cs.at[d], cr.at[d], w.partner())
        )
    for d in order:
        z = w.zd(d)
        remote(cbuf.at[d], cbuf.at[d], cs.at[d], cr.at[d], w.partner()).wait_recv()
        for e in (2, 1, 3):
            y = w.yd(e)
            both = g[z // 4, y, w.core, z % 4].astype(F32) + cbuf[d, y].astype(F32)
            psrc[e - 1, d] = both.astype(BF16)
            late.append(
                send(psrc.at[e - 1, d], ybuf.at[e - 1, d], ys.at[e - 1, d], yr.at[e - 1, d], w.at(y=y))
            )
        acc[d] = g[z // 4, w.y, w.core, z % 4].astype(F32) + cbuf[d, w.y].astype(F32)
    segments[0]()
    total = None
    for d in order:
        total = acc[d]
        for e in (1, 3, 2):
            remote(
                ybuf.at[e - 1, d], ybuf.at[e - 1, d], ys.at[e - 1, d], yr.at[e - 1, d], w.partner()
            ).wait_recv()
            total = total + ybuf[e - 1, d].astype(F32)
        if d > 0:
            zsrc[d - 1] = total.astype(BF16)
            late.append(
                send(zsrc.at[d - 1], zbuf.at[d - 1], zs.at[d - 1], zr.at[d - 1], w.at(z=w.zd(d)))
            )
    acc[0] = total
    segments[1]()
    total = acc[0]
    for d in NEAR:
        remote(
            zbuf.at[d - 1], zbuf.at[d - 1], zs.at[d - 1], zr.at[d - 1], w.partner()
        ).wait_recv()
        total = total + zbuf[d - 1].astype(F32)
    xt[w.x] = total.astype(BF16)
    for e in (2, 1, 3):
        late.append(
            send(xt.at[w.x], xt.at[w.x], xs.at[e - 1], xr.at[e - 1], w.at(x=w.xd(e)))
        )
    segments[2]()
    for e in (1, 3, 2):
        t = xt.at[w.xd(4 - e)]
        remote(t, t, xs.at[e - 1], xr.at[e - 1], w.partner()).wait_recv()
    total = xt[0].astype(F32) + xt[1].astype(F32) + xt[2].astype(F32) + xt[3].astype(F32)
    return total, late


RS_SEMS = [(8,), (8,), (3, 8), (3, 8), (7,), (7,), (3,), (3,)]
RS_BUFS = [
    pltpu.VMEM((8, 4, 16, D), BF16),
    pltpu.VMEM((3, 8, 16, D), BF16),
    pltpu.VMEM((3, 8, 16, D), BF16),
    pltpu.VMEM((8, 16, D), F32),
    pltpu.VMEM((7, 16, D), BF16),
    pltpu.VMEM((7, 16, D), BF16),
    pltpu.VMEM((4, 16, D), BF16),
]


SHIFT = (6, 2)


def dot(a, b):
    return jnp.dot(a, b, preferred_element_type=F32)


def dot_nt(a, b):
    return lax.dot_general(a, b, (((1,), (1,)), ((), ())), preferred_element_type=F32)


def dot_tn(a, b):
    return lax.dot_general(a, b, (((0,), (0,)), ((), ())), preferred_element_type=F32)


def selectors(idx_row):
    wide = jnp.broadcast_to(idx_row, (BLOCK, BLOCK))
    col = wide.T
    lane = lax.broadcasted_iota(I32, (BLOCK, BLOCK), 1)
    picks = [jnp.where(col == lane + BLOCK * j, 1.0, 0.0) for j in range(4)]
    pick = jnp.concatenate(picks, axis=1).astype(BF16)
    row = lax.broadcasted_iota(I32, (D, BLOCK), 0)
    put = jnp.where(row == jnp.broadcast_to(idx_row, (D, BLOCK)), 1.0, 0.0).astype(BF16)
    return pick, put


def block(b):
    return slice(b * BLOCK, (b + 1) * BLOCK)


def pick_rows(index_of, table, out, put, base):
    for b in range(EB):
        pick, place = selectors(index_of(b))
        out[block(b), :] = dot(pick, table[...]).astype(BF16)
        put[:, base + b * BLOCK : base + (b + 1) * BLOCK] = place


def as_column(row):
    return jnp.broadcast_to(row, (BLOCK, D)).T


def as_row(col):
    return jnp.broadcast_to(col, (D, BLOCK)).T[0:1, :]


def row_update(table, state_row, grad):
    state = as_column(state_row)[:, 0:1] + jnp.mean(grad * grad, axis=1, keepdims=True)
    return table - grad * (RATE_ROWS / (jnp.sqrt(state) + EPSILON)), state


def relation_step(rel, state, grad):
    state = state + grad * grad
    return rel - RATE_RELATIONS * grad / (jnp.sqrt(state) + EPSILON), state


def kernel(
    rel4_in, st4_in, head_in, hstate_in, tail_in, tstate_in,
    hrows_in, trows_in, negs_in, rids_in, counts_in,
    head_out, tail_out, rel_out,
    rel4, st4, head, hstate, tail, tstate, hrows, trows, negs, rids, counts,
    rel8, st8, xsrc, xbuf, rel16, st16, rel_a, rel_b, g_a, g_b,
    hb, tb, h, ht, t, n, u, gu, gn, hput, tput, terms, tnew, tmoved, tsnew, tsmoved,
    load, xsem_s, xsem_r, msem_s, msem_r, hop, hop_s, hop_r, *more,
):
    rs_bufs = [more[0:7], more[7:14]]
    more = more[14:]
    ag_sems = [more[0:6], more[6:12]]
    rs_sems = [more[12:20], more[20:28]]
    w = Place()
    barrier, peers = signal_peers(w)
    ins = (rel4_in, st4_in, hrows_in, head_in, rids_in, counts_in, tail_in, trows_in, negs_in,
           hstate_in, tstate_in)
    outs = (rel4, st4, hrows, head, rids, counts, tail, trows, negs, hstate, tstate)
    loads = []
    for i, (a, b) in enumerate(zip(ins, outs)):
        copy = pltpu.make_async_copy(a, b, load.at[i])
        copy.start()
        loads.append(copy)

    def loaded(*which):
        for i in which:
            loads[i].wait()

    def pick_head(k):
        hb[...] = head[...].astype(BF16)
        pick_rows(lambda b: hrows[k : k + 1, block(b)], hb, h, hput, 0)
        ht[...] = dot_tn(hb[...], hput[...]).astype(BF16)

    def pick_tail(k):
        pick_rows(lambda b: trows[k : k + 1, block(b)], tb, t, tput, 0)

    def pick_negs(k):
        pick_rows(lambda b: negs[k, b : b + 1, :], tb, n, tput, D)

    def score(k, rel, g):
        r0, r1 = rel[0].reshape(D, D), rel[1].reshape(D, D)
        ub, gp, gnb = [], [], []
        for b in range(EB):
            chosen = jnp.where(rids[k, b] == 1, r1, r0)
            ub.append(dot(h[block(b), :], chosen).astype(BF16))
        neg = [dot_nt(ub[b], n[block(b), :]) for b in range(EB)]
        for b in range(EB):
            u[block(b), :] = ub[b]
            live = (b < counts[k]).astype(F32)
            gnb.append((live * jax.nn.sigmoid(neg[b]) / BLOCK).astype(BF16))
            gn[block(b), :] = gnb[b]
            pos = jnp.sum(
                ub[b].astype(F32) * t[block(b), :].astype(F32), axis=1, keepdims=True
            )
            gp.append(-live * jax.nn.sigmoid(-pos))
        back = [dot(gnb[b], n[block(b), :]) for b in range(EB)]
        for b in range(EB):
            one = (rids[k, b] == 1).astype(F32)
            gub = (gp[b] * t[block(b), :].astype(F32) + back[b]).astype(BF16).astype(F32)
            gu[block(b), 0:D] = (gub * (1.0 - one)).astype(BF16)
            gu[block(b), D:] = (gub * one).astype(BF16)
        g[0] = dot(ht[...], gu[:, 0:D]).astype(BF16).reshape(4, 2, 4, 16, D)
        g[1] = dot(ht[...], gu[:, D:]).astype(BF16).reshape(4, 2, 4, 16, D)
        for b in range(EB):
            terms[block(b), :] = (gp[b] * ub[b].astype(F32)).astype(BF16)

    def tail_grad():
        for b in range(EB):
            rows = block(b)
            terms[D + b * BLOCK : D + (b + 1) * BLOCK, :] = dot_tn(gn[rows, :], u[rows, :]).astype(BF16)
        return dot(tput[...], terms[...])

    def head_grad(rel):
        r0, r1 = rel[0].reshape(D, D), rel[1].reshape(D, D)
        hterms = dot_nt(gu[:, 0:D], r0) + dot_nt(gu[:, D:], r1)
        return dot(hput[...], hterms.astype(BF16))

    nothing = lambda: None

    loaded(0, 1)
    rel8[0:4, :] = rel4[...]
    rel8[4:8, :] = rel4[...]
    st8[0:4, :] = st4[...]
    st8[4:8, :] = st4[...]
    mine = lax.broadcasted_iota(I32, (8, D), 0) // 4 == w.x % 2
    xsrc[0] = jnp.where(mine, rel8[...], 0.0)
    xsrc[1] = jnp.where(mine, st8[...], 0.0)
    pl.semaphore_wait(barrier, peers)
    xsends = []
    for part in range(2):
        for e in (2, 1, 3):
            xsends.append(
                send(
                    xsrc.at[part], xbuf.at[part, w.x],
                    xsem_s.at[part, e - 1], xsem_r.at[part, e - 1], w.at(x=w.xd(e)),
                )
            )
        xbuf[part, w.x] = xsrc[part]
    loaded(2, 3)
    pick_head(0)
    loaded(6, 7)
    tb[...] = tail[...].astype(BF16)
    pick_tail(0)

    def merge(part, out):
        for e in (1, 3, 2):
            to = xbuf.at[part, w.xd(4 - e)]
            remote(
                to, to, xsem_s.at[part, e - 1], xsem_r.at[part, e - 1], w.partner()
            ).wait_recv()
        out[0:8, :] = xbuf[part, 0] + xbuf[part, 1]
        out[8:16, :] = xbuf[part, 2] + xbuf[part, 3]

    merge(0, rel16)
    rel_a[w.z // 4, w.y, w.core, w.z % 4] = rel16[...].astype(BF16)

    def negs_first():
        loaded(8)
        pick_negs(0)

    gather_tiles(w, rel_a, ag_sems[0], (negs_first, nothing, nothing))
    loaded(4, 5, 9, 10)

    score(0, rel_a, g_a)
    def rows_of(c):
        return pl.ds(pl.multiple_of(c * 64, 64), 64)

    def chunk(c):
        part = slice(c * 64, (c + 1) * 64)
        return remote(tnew.at[part], tmoved.at[part], msem_s.at[c], msem_r.at[c], w.right)

    def shift(first, last):
        @pl.when(w.x < 3)
        def _():
            for c in range(first, last):
                chunk(c).start()

    def shift_far():
        @pl.when(w.x == 3)
        def _():
            for c in (0, 1, 2, 4, 5, 6):
                part = slice(c * 64, (c + 1) * 64)
                remote(
                    tnew.at[part], hop.at[c // 4], msem_s.at[c], hop_r.at[c // 4], w.row[c % 4]
                ).start()

    def relayed(i):
        c = w.x + 4 * i
        return remote(hop.at[i], tmoved.at[rows_of(c)], hop_s.at[i], msem_r.at[c], w.next_first)

    def relay(which):
        @pl.when(w.x == 3)
        def _():
            for i in which:
                chunk(3 + 4 * i).start()

        @pl.when(w.x < 3)
        def _():
            for i in which:
                remote(hop.at[i], hop.at[i], hop_s.at[i], hop_r.at[i], w.right).wait_recv()
                relayed(i).start()

    def tail_step():
        new, state = row_update(tail[...], tstate[...], tail_grad())
        tnew[...] = new.astype(BF16)
        tsnew[...] = as_row(state)
        send(tsnew, tsmoved, msem_s.at[8], msem_r.at[8], w.right)
        shift_far()
        shift(0, SHIFT[0])

    def head_step():
        new, state = row_update(head[...], hstate[...], head_grad(rel_a))
        head[...] = new
        hstate[...] = as_row(state)

    def head_again():
        shift(SHIFT[0], 8)
        pick_head(1)

    grad, late = reduce_tiles(
        w, g_a, rs_bufs[0], rs_sems[0], (tail_step, head_step, head_again)
    )
    merge(1, st16)
    new, state = relation_step(rel16[...], st16[...], grad)
    rel16[...] = new
    st16[...] = state
    rel_b[w.z // 4, w.y, w.core, w.z % 4] = new.astype(BF16)

    def tail_arrives():
        for c in range(8):
            chunk(c).wait()

        @pl.when(w.x < 3)
        def _():
            for i in range(2):
                relayed(i).wait_send()

        remote(tsnew, tsmoved, msem_s.at[8], msem_r.at[8], w.right).wait()
        pick_rows(lambda b: trows[1:2, block(b)], tmoved, t, tput, 0)
        pick_rows(lambda b: negs[1, b : b + 1, :], tmoved, n, tput, D)

    gather_tiles(
        w, rel_b, ag_sems[1],
        (lambda: relay((0, 1)), tail_arrives, nothing),
    )

    score(1, rel_b, g_b)

    def tail_last():
        new, _ = row_update(tmoved[...].astype(F32), tsmoved[...], tail_grad())
        tail_out[...] = new

    def head_last():
        new, _ = row_update(head[...], hstate[...], head_grad(rel_b))
        head_out[...] = new

    grad, later = reduce_tiles(
        w, g_b, rs_bufs[1], rs_sems[1], (tail_last, head_last, nothing)
    )
    new, _ = relation_step(rel16[...], st16[...], grad)
    out = new[0:4]
    for i in range(1, 4):
        out = jnp.where(w.x == i, new[4 * i : 4 * i + 4], out)
    rel_out[...] = out
    for copy in xsends + late + later:
        copy.wait_send()


def store(a, b, c, a_out, b_out, c_out, sems):
    copies = [
        pltpu.make_async_copy(x, y, sems.at[i])
        for i, (x, y) in enumerate(((a, a_out), (b, b_out), (c, c_out)))
    ]
    for copy in copies:
        copy.start()
    for copy in copies:
        copy.wait()


def dma(shape):
    return pltpu.SemaphoreType.DMA(shape)


def shards(
    head_table,
    head_state,
    tail_table,
    tail_state,
    relations,
    relation_state,
    head_rows,
    tail_rows,
    negatives,
    relation_ids,
    block_counts,
):
    table = jax.ShapeDtypeStruct((D, D), F32)
    args = (
        relations, relation_state, head_table, head_state.reshape(1, D), tail_table,
        tail_state.reshape(1, D), head_rows, tail_rows, negatives, relation_ids,
        block_counts.reshape(2),
    )
    args = tuple(pltpu.with_memory_space_constraint(a, pltpu.HBM) for a in args)
    square = pltpu.VMEM((D, D), BF16)
    big = pltpu.VMEM((2, 4, 2, 4, 16, D), BF16)
    scratch = [
        pltpu.VMEM((4, D), F32),
        pltpu.VMEM((4, D), F32),
        pltpu.VMEM((D, D), F32),
        pltpu.VMEM((1, D), F32),
        pltpu.VMEM((D, D), F32),
        pltpu.VMEM((1, D), F32),
        pltpu.VMEM((2, D), I32),
        pltpu.VMEM((2, D), I32),
        pltpu.VMEM((2, EB, BLOCK), I32),
        pltpu.SMEM((2, EB), I32),
        pltpu.SMEM((2,), I32),
        pltpu.VMEM((8, D), F32),
        pltpu.VMEM((8, D), F32),
        pltpu.VMEM((2, 8, D), F32),
        pltpu.VMEM((2, 4, 8, D), F32),
        pltpu.VMEM((16, D), F32),
        pltpu.VMEM((16, D), F32),
        big, big, big, big,
        square, square, square, square, square, square, square,
        pltpu.VMEM((D, 2 * D), BF16),
        pltpu.VMEM((D, BLOCK), BF16),
        square,
        pltpu.VMEM((D, 2 * D), BF16),
        pltpu.VMEM((2 * D, D), BF16),
        square, square,
        pltpu.VMEM((1, D), F32),
        pltpu.VMEM((1, D), F32),
        dma((11,)), dma((2, 3)), dma((2, 3)), dma((9,)), dma((9,)),
        pltpu.VMEM((2, 64, D), BF16), dma((2,)), dma((2,)),
    ]
    scratch += RS_BUFS + RS_BUFS
    scratch += [dma(s) for s in AG_SEMS + AG_SEMS + RS_SEMS + RS_SEMS]
    results = pl.pallas_call(
        kernel,
        name="rescal",
        out_shape=(table, table, jax.ShapeDtypeStruct((4, D), F32)),
        in_specs=[ANY] * len(args),
        out_specs=[VMEM] * 3,
        scratch_shapes=scratch,
        compiler_params=pltpu.CompilerParams(
            collective_id=1, has_side_effects=True, vmem_limit_bytes=30 << 20
        ),
    )(*args)
    return pl.pallas_call(
        store,
        name="store",
        out_shape=(table, table, jax.ShapeDtypeStruct((4, D), F32)),
        in_specs=[VMEM] * 3,
        out_specs=[ANY] * 3,
        scratch_shapes=[dma((3,))],
        compiler_params=pltpu.CompilerParams(vmem_limit_bytes=8 << 20),
    )(*results)


def solution(mesh):
    both = ("head", "tail")
    in_specs = (
        P(both, None),
        P(both),
        P(both, None),
        P(both),
        P(both, None),
        P(both, None),
        P(None, both),
        P(None, both),
        P(None, both, None),
        P(None, both),
        P(None, both),
    )
    out_specs = (P(both, None), P(both, None), P(both, None))
    return jax.shard_map(shards, mesh=mesh, in_specs=in_specs, out_specs=out_specs, check_vma=False)
```

```python
import jax
import jax.numpy as jnp
from jax import lax
from jax.experimental import pallas as pl
from jax.experimental.pallas import tpu as pltpu
from jax.sharding import PartitionSpec as P

MESH = pl.DeviceIdType.MESH
RATE_ROWS = 0.2
RATE_RELATIONS = 0.05
EPSILON = 1e-06
D = 512
EB = 4
BLOCK = 128
F32 = jnp.float32
BF16 = jnp.bfloat16
I32 = jnp.int32
VMEM = pl.BlockSpec(memory_space=pltpu.VMEM)
ANY = pl.BlockSpec(memory_space=pltpu.HBM)


class Place:
    def __init__(self):
        hd, tl = lax.axis_index("head"), lax.axis_index("tail")
        self.core, self.y, self.x = hd % 2, (hd // 2) % 4, tl % 4
        self.z = (hd // 8) * 4 + tl // 4
        self.right, self.left = (hd, (tl + 1) % 16), (hd, (tl + 15) % 16)
        self.row = [(hd, tl - self.x + r) for r in range(4)]
        self.next_first = (hd, (tl - self.x + 4) % 16)
        self.row_before = [(hd, (tl - self.x + 12 + r) % 16) for r in range(4)]

    def at(self, core=None, y=None, z=None, x=None):
        core = self.core if core is None else core
        y = self.y if y is None else y
        z = self.z if z is None else z
        x = self.x if x is None else x
        return ((z // 4) * 8 + y * 2 + core, (z % 4) * 4 + x)

    def partner(self):
        return self.at(core=1 - self.core)

    def xd(self, d):
        return (self.x + d) % 4

    def yd(self, d):
        return (self.y + d) % 4

    def zd(self, d):
        return (self.z + d) % 8


NEAR = (1, 7, 2, 6, 3, 5, 4)
FAR = (4, 3, 5, 2, 6, 1, 7)


def signal_peers(w):
    barrier = pltpu.get_barrier_semaphore()
    peers = [w.at(z=w.zd(d)) for d in FAR] + [w.right, w.left]
    peers += [w.at(y=w.yd(d)) for d in (2, 1, 3)] + [w.at(x=w.xd(d)) for d in (2, 1, 3)]
    peers.append(w.partner())
    for peer in peers:
        pl.semaphore_signal(barrier, inc=1, device_id=peer, device_id_type=MESH)

    @pl.when(w.x == 0)
    def _():
        for r in (1, 2):
            pl.semaphore_signal(
                barrier, inc=1, device_id=w.row_before[r], device_id_type=MESH
            )

    @pl.when((w.x == 1) | (w.x == 2))
    def _():
        pl.semaphore_signal(barrier, inc=1, device_id=w.next_first, device_id_type=MESH)

    extra = jnp.where(w.x == 0, 2, jnp.where(w.x == 3, 0, 1))
    return barrier, len(peers) + extra


def remote(src, dst, ssem, rsem, to):
    return pltpu.make_async_remote_copy(
        src_ref=src, dst_ref=dst, send_sem=ssem, recv_sem=rsem, device_id=to, device_id_type=MESH
    )


def send(src, dst, ssem, rsem, to):
    copy = remote(src, dst, ssem, rsem, to)
    copy.start()
    return copy


def gather_tiles(w, rel, sems, segments):
    zs, zr, ys, yr, cs, cr = sems
    late = []

    def tile(z, y, core):
        return rel.at[z // 4, y, core, z % 4]

    def to_core(t):
        send(t, t, cs.at[0], cr.at[0], w.partner())

    def spread(d):
        t = tile(w.zd(8 - d), w.y, w.core)
        for e in (2, 1, 3):
            late.append(send(t, t, ys.at[e - 1, d], yr.at[e - 1, d], w.at(y=w.yd(e))))

    def arrive_z(d):
        t = tile(w.zd(8 - d), w.y, w.core)
        remote(t, t, zs.at[d - 1], zr.at[d - 1], w.partner()).wait_recv()
        spread(d)

    def arrive_y(d):
        for e in (1, 3, 2):
            t = tile(w.zd(8 - d), w.yd(4 - e), w.core)
            remote(t, t, ys.at[e - 1, d], yr.at[e - 1, d], w.partner()).wait_recv()
        z = w.zd(8 - d)
        to_core(rel.at[z // 4, :, w.core, z % 4])

    own = tile(w.z, w.y, w.core)
    for d in FAR:
        late.append(send(own, own, zs.at[d - 1], zr.at[d - 1], w.at(z=w.zd(d))))
    spread(0)
    segments[0]()
    for d in (1, 7, 2, 6):
        arrive_z(d)
    segments[2]()
    arrive_y(0)
    arrive_z(3)
    arrive_z(5)
    arrive_z(4)
    segments[1]()
    for d in NEAR:
        arrive_y(d)
    other = rel.at[:, :, 1 - w.core]
    half = rel.at[:, :, w.core]
    remote(other, other, cs.at[0], cr.at[0], w.partner()).wait_recv()
    remote(half, half, cs.at[0], cr.at[0], w.partner()).wait_send()
    for copy in late:
        copy.wait_send()


AG_SEMS = [(7,), (7,), (3, 8), (3, 8), (1,), (1,)]


def reduce_tiles(w, g, bufs, sems, segments):
    cbuf, psrc, ybuf, acc, zsrc, zbuf, xt = bufs
    cs, cr, ys, yr, zs, zr, xs, xr = sems
    late = []
    order = FAR + (0,)
    for d in order:
        z = w.zd(d)
        late.append(
            send(g.at[z // 4, :, 1 - w.core, z % 4], cbuf.at[d], cs.at[d], cr.at[d], w.partner())
        )
    for d in order:
        z = w.zd(d)
        remote(cbuf.at[d], cbuf.at[d], cs.at[d], cr.at[d], w.partner()).wait_recv()
        for e in (2, 1, 3):
            y = w.yd(e)
            both = g[z // 4, y, w.core, z % 4].astype(F32) + cbuf[d, y].astype(F32)
            psrc[e - 1, d] = both.astype(BF16)
            late.append(
                send(psrc.at[e - 1, d], ybuf.at[e - 1, d], ys.at[e - 1, d], yr.at[e - 1, d], w.at(y=y))
            )
        acc[d] = g[z // 4, w.y, w.core, z % 4].astype(F32) + cbuf[d, w.y].astype(F32)
    segments[0]()
    total = None
    for d in order:
        total = acc[d]
        for e in (1, 3, 2):
            remote(
                ybuf.at[e - 1, d], ybuf.at[e - 1, d], ys.at[e - 1, d], yr.at[e - 1, d], w.partner()
            ).wait_recv()
            total = total + ybuf[e - 1, d].astype(F32)
        if d > 0:
            zsrc[d - 1] = total.astype(BF16)
            late.append(
                send(zsrc.at[d - 1], zbuf.at[d - 1], zs.at[d - 1], zr.at[d - 1], w.at(z=w.zd(d)))
            )
    acc[0] = total
    segments[1]()
    total = acc[0]
    for d in NEAR:
        remote(
            zbuf.at[d - 1], zbuf.at[d - 1], zs.at[d - 1], zr.at[d - 1], w.partner()
        ).wait_recv()
        total = total + zbuf[d - 1].astype(F32)
    xt[w.x] = total.astype(BF16)
    for e in (2, 1, 3):
        late.append(
            send(xt.at[w.x], xt.at[w.x], xs.at[e - 1], xr.at[e - 1], w.at(x=w.xd(e)))
        )
    segments[2]()
    for e in (1, 3, 2):
        t = xt.at[w.xd(4 - e)]
        remote(t, t, xs.at[e - 1], xr.at[e - 1], w.partner()).wait_recv()
    total = xt[0].astype(F32) + xt[1].astype(F32) + xt[2].astype(F32) + xt[3].astype(F32)
    return total, late


RS_SEMS = [(8,), (8,), (3, 8), (3, 8), (7,), (7,), (3,), (3,)]
RS_BUFS = [
    pltpu.VMEM((8, 4, 16, D), BF16),
    pltpu.VMEM((3, 8, 16, D), BF16),
    pltpu.VMEM((3, 8, 16, D), BF16),
    pltpu.VMEM((8, 16, D), F32),
    pltpu.VMEM((7, 16, D), BF16),
    pltpu.VMEM((7, 16, D), BF16),
    pltpu.VMEM((4, 16, D), BF16),
]


SHIFT = (6, 2)


def dot(a, b):
    return jnp.dot(a, b, preferred_element_type=F32)


def dot_nt(a, b):
    return lax.dot_general(a, b, (((1,), (1,)), ((), ())), preferred_element_type=F32)


def dot_tn(a, b):
    return lax.dot_general(a, b, (((0,), (0,)), ((), ())), preferred_element_type=F32)


def selectors(idx_row):
    wide = jnp.broadcast_to(idx_row, (BLOCK, BLOCK))
    col = wide.T
    lane = lax.broadcasted_iota(I32, (BLOCK, BLOCK), 1)
    picks = [jnp.where(col == lane + BLOCK * j, 1.0, 0.0) for j in range(4)]
    pick = jnp.concatenate(picks, axis=1).astype(BF16)
    row = lax.broadcasted_iota(I32, (D, BLOCK), 0)
    put = jnp.where(row == jnp.broadcast_to(idx_row, (D, BLOCK)), 1.0, 0.0).astype(BF16)
    return pick, put


def block(b):
    return slice(b * BLOCK, (b + 1) * BLOCK)


def pick_rows(index_of, table, out, put, base):
    for b in range(EB):
        pick, place = selectors(index_of(b))
        out[block(b), :] = dot(pick, table[...]).astype(BF16)
        put[:, base + b * BLOCK : base + (b + 1) * BLOCK] = place


def as_column(row):
    return jnp.broadcast_to(row, (BLOCK, D)).T


def as_row(col):
    return jnp.broadcast_to(col, (D, BLOCK)).T[0:1, :]


def row_update(table, state_row, grad):
    state = as_column(state_row)[:, 0:1] + jnp.mean(grad * grad, axis=1, keepdims=True)
    return table - grad * (RATE_ROWS / (jnp.sqrt(state) + EPSILON)), state


def relation_step(rel, state, grad):
    state = state + grad * grad
    return rel - RATE_RELATIONS * grad / (jnp.sqrt(state) + EPSILON), state


def kernel(
    rel4_in, st4_in, head_in, hstate_in, tail_in, tstate_in,
    hrows_in, trows_in, negs_in, rids_in, counts_in,
    head_out, tail_out, rel_out,
    rel4, st4, head, hstate, tail, tstate, hrows, trows, negs, rids, counts,
    rel8, st8, xsrc, xbuf, rel16, st16, rel_a, rel_b, g_a, g_b,
    hb, tb, h, ht, t, n, u, gu, gn, hput, tput, terms, tnew, tmoved, tsnew, tsmoved,
    load, xsem_s, xsem_r, msem_s, msem_r, hop, hop_s, hop_r, *more,
):
    rs_bufs = [more[0:7], more[7:14]]
    more = more[14:]
    ag_sems = [more[0:6], more[6:12]]
    rs_sems = [more[12:20], more[20:28]]
    w = Place()
    barrier, peers = signal_peers(w)
    ins = (rel4_in, st4_in, hrows_in, head_in, rids_in, counts_in, tail_in, trows_in, negs_in,
           hstate_in, tstate_in)
    outs = (rel4, st4, hrows, head, rids, counts, tail, trows, negs, hstate, tstate)
    loads = []
    for i, (a, b) in enumerate(zip(ins, outs)):
        copy = pltpu.make_async_copy(a, b, load.at[i])
        copy.start()
        loads.append(copy)

    def loaded(*which):
        for i in which:
            loads[i].wait()

    def pick_head(k):
        hb[...] = head[...].astype(BF16)
        pick_rows(lambda b: hrows[k : k + 1, block(b)], hb, h, hput, 0)
        ht[...] = dot_tn(hb[...], hput[...]).astype(BF16)

    def pick_tail(k):
        pick_rows(lambda b: trows[k : k + 1, block(b)], tb, t, tput, 0)

    def pick_negs(k):
        pick_rows(lambda b: negs[k, b : b + 1, :], tb, n, tput, D)

    def score(k, rel, g):
        r0, r1 = rel[0].reshape(D, D), rel[1].reshape(D, D)
        ub, gp, gnb = [], [], []
        for b in range(EB):
            chosen = jnp.where(rids[k, b] == 1, r1, r0)
            ub.append(dot(h[block(b), :], chosen).astype(BF16))
        neg = [dot_nt(ub[b], n[block(b), :]) for b in range(EB)]
        for b in range(EB):
            u[block(b), :] = ub[b]
            live = (b < counts[k]).astype(F32)
            gnb.append((live * jax.nn.sigmoid(neg[b]) / BLOCK).astype(BF16))
            gn[block(b), :] = gnb[b]
            pos = jnp.sum(
                ub[b].astype(F32) * t[block(b), :].astype(F32), axis=1, keepdims=True
            )
            gp.append(-live * jax.nn.sigmoid(-pos))
        back = [dot(gnb[b], n[block(b), :]) for b in range(EB)]
        for b in range(EB):
            one = (rids[k, b] == 1).astype(F32)
            gub = (gp[b] * t[block(b), :].astype(F32) + back[b]).astype(BF16).astype(F32)
            gu[block(b), 0:D] = (gub * (1.0 - one)).astype(BF16)
            gu[block(b), D:] = (gub * one).astype(BF16)
        g[0] = dot(ht[...], gu[:, 0:D]).astype(BF16).reshape(4, 2, 4, 16, D)
        g[1] = dot(ht[...], gu[:, D:]).astype(BF16).reshape(4, 2, 4, 16, D)
        for b in range(EB):
            terms[block(b), :] = (gp[b] * ub[b].astype(F32)).astype(BF16)

    def tail_grad():
        for b in range(EB):
            rows = block(b)
            terms[D + b * BLOCK : D + (b + 1) * BLOCK, :] = dot_tn(gn[rows, :], u[rows, :]).astype(BF16)
        return dot(tput[...], terms[...])

    def head_grad(rel):
        r0, r1 = rel[0].reshape(D, D), rel[1].reshape(D, D)
        hterms = dot_nt(gu[:, 0:D], r0) + dot_nt(gu[:, D:], r1)
        return dot(hput[...], hterms.astype(BF16))

    nothing = lambda: None

    loaded(0, 1)
    rel8[0:4, :] = rel4[...]
    rel8[4:8, :] = rel4[...]
    st8[0:4, :] = st4[...]
    st8[4:8, :] = st4[...]
    mine = lax.broadcasted_iota(I32, (8, D), 0) // 4 == w.x % 2
    xsrc[0] = jnp.where(mine, rel8[...], 0.0)
    xsrc[1] = jnp.where(mine, st8[...], 0.0)
    pl.semaphore_wait(barrier, peers)
    xsends = []
    for part in range(2):
        for e in (2, 1, 3):
            xsends.append(
                send(
                    xsrc.at[part], xbuf.at[part, w.x],
                    xsem_s.at[part, e - 1], xsem_r.at[part, e - 1], w.at(x=w.xd(e)),
                )
            )
        xbuf[part, w.x] = xsrc[part]
    loaded(2, 3)
    pick_head(0)

    def merge(part, out):
        for e in (1, 3, 2):
            to = xbuf.at[part, w.xd(4 - e)]
            remote(
                to, to, xsem_s.at[part, e - 1], xsem_r.at[part, e - 1], w.partner()
            ).wait_recv()
        out[0:8, :] = xbuf[part, 0] + xbuf[part, 1]
        out[8:16, :] = xbuf[part, 2] + xbuf[part, 3]

    merge(0, rel16)
    rel_a[w.z // 4, w.y, w.core, w.z % 4] = rel16[...].astype(BF16)

    def negs_first():
        loaded(6, 7, 8)
        tb[...] = tail[...].astype(BF16)
        pick_tail(0)
        pick_negs(0)

    gather_tiles(w, rel_a, ag_sems[0], (negs_first, nothing, nothing))
    loaded(4, 5, 9, 10)

    score(0, rel_a, g_a)
    def rows_of(c):
        return pl.ds(pl.multiple_of(c * 64, 64), 64)

    def chunk(c):
        part = slice(c * 64, (c + 1) * 64)
        return remote(tnew.at[part], tmoved.at[part], msem_s.at[c], msem_r.at[c], w.right)

    def shift(first, last):
        @pl.when(w.x < 3)
        def _():
            for c in range(first, last):
                chunk(c).start()

    def shift_far():
        @pl.when(w.x == 3)
        def _():
            for c in (0, 1, 2, 4, 5, 6):
                part = slice(c * 64, (c + 1) * 64)
                remote(
                    tnew.at[part], hop.at[c // 4], msem_s.at[c], hop_r.at[c // 4], w.row[c % 4]
                ).start()

    def relayed(i):
        c = w.x + 4 * i
        return remote(hop.at[i], tmoved.at[rows_of(c)], hop_s.at[i], msem_r.at[c], w.next_first)

    def relay(which):
        @pl.when(w.x == 3)
        def _():
            for i in which:
                chunk(3 + 4 * i).start()

        @pl.when(w.x < 3)
        def _():
            for i in which:
                remote(hop.at[i], hop.at[i], hop_s.at[i], hop_r.at[i], w.right).wait_recv()
                relayed(i).start()

    def tail_step():
        new, state = row_update(tail[...], tstate[...], tail_grad())
        tnew[...] = new.astype(BF16)
        tsnew[...] = as_row(state)
        send(tsnew, tsmoved, msem_s.at[8], msem_r.at[8], w.right)
        shift_far()
        shift(0, SHIFT[0])

    def head_step():
        new, state = row_update(head[...], hstate[...], head_grad(rel_a))
        head[...] = new
        hstate[...] = as_row(state)

    def head_again():
        shift(SHIFT[0], 8)
        pick_head(1)

    grad, late = reduce_tiles(
        w, g_a, rs_bufs[0], rs_sems[0], (tail_step, head_step, head_again)
    )
    merge(1, st16)
    new, state = relation_step(rel16[...], st16[...], grad)
    rel16[...] = new
    st16[...] = state
    rel_b[w.z // 4, w.y, w.core, w.z % 4] = new.astype(BF16)

    def tail_arrives():
        for c in range(8):
            chunk(c).wait()

        @pl.when(w.x < 3)
        def _():
            for i in range(2):
                relayed(i).wait_send()

        remote(tsnew, tsmoved, msem_s.at[8], msem_r.at[8], w.right).wait()
        pick_rows(lambda b: trows[1:2, block(b)], tmoved, t, tput, 0)
        pick_rows(lambda b: negs[1, b : b + 1, :], tmoved, n, tput, D)

    gather_tiles(
        w, rel_b, ag_sems[1],
        (lambda: relay((0, 1)), tail_arrives, nothing),
    )

    score(1, rel_b, g_b)

    def tail_last():
        new, _ = row_update(tmoved[...].astype(F32), tsmoved[...], tail_grad())
        tail_out[...] = new

    def head_last():
        new, _ = row_update(head[...], hstate[...], head_grad(rel_b))
        head_out[...] = new

    grad, later = reduce_tiles(
        w, g_b, rs_bufs[1], rs_sems[1], (tail_last, head_last, nothing)
    )
    new, _ = relation_step(rel16[...], st16[...], grad)
    out = new[0:4]
    for i in range(1, 4):
        out = jnp.where(w.x == i, new[4 * i : 4 * i + 4], out)
    rel_out[...] = out
    for copy in xsends + late + later:
        copy.wait_send()


def store(a, b, c, a_out, b_out, c_out, sems):
    copies = [
        pltpu.make_async_copy(x, y, sems.at[i])
        for i, (x, y) in enumerate(((a, a_out), (b, b_out), (c, c_out)))
    ]
    for copy in copies:
        copy.start()
    for copy in copies:
        copy.wait()


def dma(shape):
    return pltpu.SemaphoreType.DMA(shape)


def shards(
    head_table,
    head_state,
    tail_table,
    tail_state,
    relations,
    relation_state,
    head_rows,
    tail_rows,
    negatives,
    relation_ids,
    block_counts,
):
    table = jax.ShapeDtypeStruct((D, D), F32)
    args = (
        relations, relation_state, head_table, head_state.reshape(1, D), tail_table,
        tail_state.reshape(1, D), head_rows, tail_rows, negatives, relation_ids,
        block_counts.reshape(2),
    )
    args = tuple(pltpu.with_memory_space_constraint(a, pltpu.HBM) for a in args)
    square = pltpu.VMEM((D, D), BF16)
    big = pltpu.VMEM((2, 4, 2, 4, 16, D), BF16)
    scratch = [
        pltpu.VMEM((4, D), F32),
        pltpu.VMEM((4, D), F32),
        pltpu.VMEM((D, D), F32),
        pltpu.VMEM((1, D), F32),
        pltpu.VMEM((D, D), F32),
        pltpu.VMEM((1, D), F32),
        pltpu.VMEM((2, D), I32),
        pltpu.VMEM((2, D), I32),
        pltpu.VMEM((2, EB, BLOCK), I32),
        pltpu.SMEM((2, EB), I32),
        pltpu.SMEM((2,), I32),
        pltpu.VMEM((8, D), F32),
        pltpu.VMEM((8, D), F32),
        pltpu.VMEM((2, 8, D), F32),
        pltpu.VMEM((2, 4, 8, D), F32),
        pltpu.VMEM((16, D), F32),
        pltpu.VMEM((16, D), F32),
        big, big, big, big,
        square, square, square, square, square, square, square,
        pltpu.VMEM((D, 2 * D), BF16),
        pltpu.VMEM((D, BLOCK), BF16),
        square,
        pltpu.VMEM((D, 2 * D), BF16),
        pltpu.VMEM((2 * D, D), BF16),
        square, square,
        pltpu.VMEM((1, D), F32),
        pltpu.VMEM((1, D), F32),
        dma((11,)), dma((2, 3)), dma((2, 3)), dma((9,)), dma((9,)),
        pltpu.VMEM((2, 64, D), BF16), dma((2,)), dma((2,)),
    ]
    scratch += RS_BUFS + RS_BUFS
    scratch += [dma(s) for s in AG_SEMS + AG_SEMS + RS_SEMS + RS_SEMS]
    results = pl.pallas_call(
        kernel,
        name="rescal",
        out_shape=(table, table, jax.ShapeDtypeStruct((4, D), F32)),
        in_specs=[ANY] * len(args),
        out_specs=[VMEM] * 3,
        scratch_shapes=scratch,
        compiler_params=pltpu.CompilerParams(
            collective_id=1, has_side_effects=True, vmem_limit_bytes=30 << 20
        ),
    )(*args)
    return pl.pallas_call(
        store,
        name="store",
        out_shape=(table, table, jax.ShapeDtypeStruct((4, D), F32)),
        in_specs=[VMEM] * 3,
        out_specs=[ANY] * 3,
        scratch_shapes=[dma((3,))],
        compiler_params=pltpu.CompilerParams(vmem_limit_bytes=8 << 20),
    )(*results)


def solution(mesh):
    both = ("head", "tail")
    in_specs = (
        P(both, None),
        P(both),
        P(both, None),
        P(both),
        P(both, None),
        P(both, None),
        P(None, both),
        P(None, both),
        P(None, both, None),
        P(None, both),
        P(None, both),
    )
    out_specs = (P(both, None), P(both, None), P(both, None))
    return jax.shard_map(shards, mesh=mesh, in_specs=in_specs, out_specs=out_specs, check_vma=False)
```
